32 devices in a mesh: tm: 16 (over z, y, x), col: 2 (over core).
Axes of the slice: x: 2, y: 2, z: 4, core: 2. Of those that a mesh axis runs over, the one named last changes fastest.
Arguments:
- rhs: float32 [16, 1024, 256], P('tm', 'col'), may hold values from -6 to 6
- inverse_blocks: float32 [3, 16, 1024, 1024], P(None, 'tm', None, 'col'), may hold values from -2 to 3, as said below
- lower_coupling: float32 [3, 16, 1024, 1024], P(None, 'tm', None, 'col'), may hold values from -0.1875 to 0.1875
- upper_coupling: float32 [3, 16, 1024, 1024], P(None, 'tm', None, 'col'), may hold values from -0.1875 to 0.1875
- tile_pattern: int32 [3, 16, 2, 8, 8], P(None, 'tm', None, None, 'col'), may hold values from 0 to 1, as said below
- tip_coupling: float32 [3, 16, 64, 1024], P(None, 'tm', None, 'col'), may hold values from -0.046875 to 0.046875
- tip_rhs: float32 [64, 256], replicated, may hold values from -6 to 6
Outputs:
- reduced: float32 [16, 1024, 256], P('tm', 'col')
- tip_reduced: float32 [64, 256], replicated
The draws below stay inside these ranges and needn't reach their ends.
Inputs may be any that keep to these rules, and one draw needn't show every extreme that they name: Every inverse_blocks[l, j] is symmetric. tile_pattern[l, j, k, r, c] is 1 exactly where |r - c| is at most a half-width w[l, j, k] of 1 to 4; both half-widths 1 and 4 occur.
All inputs are finite; a program needn't handle non-finite values.
Results may differ from the reference program's by a relative error of at most 0.0001.
Values sent between devices are 32-bit elements; how exact they have to be, the bound alone decides.
A program may use at most 64 MiB of HBM per device.

```python
import math
import jax
import jax.numpy as jnp
from jax import lax

B = 1024
F = 64
NT = 8
REDUCTION_DEPTH = 3
R = 256
NB = 16


def draw_inverse_blocks(key, part):
    noise_draw = jnp.clip(jax.random.normal(key, (REDUCTION_DEPTH, NB, B, B), jnp.float32), -6.0, 6.0)
    symmetric = (noise_draw + jnp.swapaxes(noise_draw, 2, 3)) * (0.1 / math.sqrt(2.0 * B))
    diagonal = jnp.exp(jax.random.uniform(jax.random.fold_in(key, 1), (REDUCTION_DEPTH, NB, B), jnp.float32, math.log(0.25), math.log(0.5)))
    blocks = symmetric + diagonal[:, :, :, None] * jnp.eye(B, dtype=jnp.float32)[None, None]
    return blocks


def draw_tile_pattern(key, part):
    widest = NT // 2
    band_width = jax.random.randint(key, (REDUCTION_DEPTH, NB, 2), 1, widest + 1)
    band_width = band_width.at[0, 0, 0].set(1).at[0, 0, 1].set(widest)
    tile_index = jnp.arange(NT)
    tile_gap = jnp.abs(tile_index[:, None] - tile_index[None, :])
    return (tile_gap[None, None, None] <= band_width[:, :, :, None, None]).astype(jnp.int32)


def levels(rng, dims, cuts, least, largest):
    level, own = 1.0, jax.random.fold_in(rng, 6)
    for position, blocks in cuts:
        steps = jnp.exp(jax.random.uniform(jax.random.fold_in(own, position), (blocks,), jnp.float32, least / len(cuts), largest / len(cuts)))
        level = level * jnp.repeat(steps, dims[position] // blocks).reshape([-1 if axis == position else 1 for axis in range(len(dims))])
    return level


def normal_values(own_key, extent, deviation, bound, shards=(), kind=jnp.bfloat16):
    level = levels(own_key, extent, shards, -0.22, 0.18) if shards else 1.0
    drawn = jax.random.normal(own_key, extent, jnp.float32) * deviation * level
    return jnp.minimum(jnp.maximum(drawn, -bound), bound).astype(kind)


def setup_inputs(seed: int = 0) -> dict:
    key_of = jax.random.split(jax.random.key(seed), 8)
    rhs = normal_values(key_of[0], (NB, B, R), 1.0, 6.0, ((0, 16), (1, 2)), jnp.float32)
    inverse_blocks = draw_inverse_blocks(jax.random.fold_in(key_of[7], 71), 0)
    lower_coupling = normal_values(key_of[2], (REDUCTION_DEPTH, NB, B, B), B ** -0.5, 0.1875, ((1, 16), (3, 2)), jnp.float32)
    upper_coupling = normal_values(key_of[3], (REDUCTION_DEPTH, NB, B, B), B ** -0.5, 0.1875, ((1, 16), (3, 2)), jnp.float32)
    tile_pattern = draw_tile_pattern(jax.random.fold_in(key_of[7], 71), 0)
    tip_coupling = normal_values(key_of[5], (REDUCTION_DEPTH, NB, F, B), (B * NB) ** -0.5, 0.046875, ((1, 16), (3, 2)), jnp.float32)
    tip_rhs = normal_values(key_of[6], (F, R), 1.0, 6.0, (), jnp.float32)
    return {"rhs": rhs, "inverse_blocks": inverse_blocks, "lower_coupling": lower_coupling, "upper_coupling": upper_coupling, "tile_pattern": tile_pattern, "tip_coupling": tip_coupling, "tip_rhs": tip_rhs}


def expand(pattern):
    tile_size = B // NT
    widened = jnp.repeat(pattern.astype(jnp.float32), tile_size, axis=1)
    return jnp.repeat(widened, tile_size, axis=2)


def reference(rhs, inverse_blocks, lower_coupling, upper_coupling, tile_pattern, tip_coupling, tip_rhs):
    highest = lax.Precision.HIGHEST
    present_rows = rhs
    tip_total = tip_rhs
    for level_number in range(REDUCTION_DEPTH):
        stride = 2 ** level_number
        lower_masked = lower_coupling[level_number] * expand(tile_pattern[level_number, :, 0])
        upper_masked = upper_coupling[level_number] * expand(tile_pattern[level_number, :, 1])
        solved = jnp.einsum("jab,jbr->jar", inverse_blocks[level_number], present_rows, precision=highest)
        down_term = jnp.einsum("jba,jbr->jar", lower_masked, solved, precision=highest)
        up_term = jnp.einsum("jba,jbr->jar", upper_masked, solved, precision=highest)
        present_rows = present_rows - jnp.roll(down_term, -stride, axis=0) - jnp.roll(up_term, stride, axis=0)
        tip_total = tip_total - jnp.einsum("jfb,jbr->fr", tip_coupling[level_number], solved, precision=highest)
    return present_rows, tip_total
```

```python
import contextlib
import functools

import jax
import jax.numpy as jnp
from jax import lax
from jax.experimental import pallas as pl
from jax.experimental.pallas import tpu as pltpu
from jax.sharding import PartitionSpec as P

MESH = pl.DeviceIdType.MESH
LANES = 128
ROWS = 8
TRACE = False
NT = (((1,), (1,)), ((), ()))
NN = (((1,), (0,)), ((), ()))


def scope(name):
    return jax.named_scope(name) if TRACE else contextlib.nullcontext()


def halves_of(x):
    high = x.astype(jnp.bfloat16)
    low = (x - high.astype(jnp.float32)).astype(jnp.bfloat16)
    return high, low


def product(stacked, high, w_high, w_low, form):
    rows = high.shape[0]
    dot = functools.partial(
        lax.dot_general, dimension_numbers=form, preferred_element_type=jnp.float32
    )
    both = dot(stacked, w_high)
    return both[:rows] + both[rows:] + dot(high, w_low)


ORDER = (
    "S00", "P01", "P02", "S01", "P03", "J00", "S02", "K00", "W20", "W12", "W11", "J01",
    "S03", "K01", "W10", "P10", "J02", "K02", "S10", "J03", "P11", "K03", "P12", "J10",
    "S11", "K10", "S12", "P13", "W21", "W22", "J11", "S13", "P20", "K11", "J12", "S20",
    "K12", "J13", "P21", "K13", "S21", "P22", "P23", "S22", "S23",
)
PIECES = 4


def pieces(R):
    return tuple((R * h // PIECES, R // PIECES) for h in range(PIECES))


def kernel(
    dims,
    rhs_hbm,
    inv_hbm,
    low_hbm,
    up_hbm,
    pattern,
    tip_c_hbm,
    tip_rhs_hbm,
    out,
    tip_out,
    rhs_v,
    tip_c,
    tip_rhs,
    raw,
    w_high,
    w_low,
    cur,
    part,
    stk,
    send,
    recv,
    joined,
    tip_acc,
    tip_near,
    tip_far,
    tip_all,
    in_sem,
    rhs_sem,
    part_s,
    part_r,
    row_s,
    row_r,
    near_s,
    near_r,
    far_s,
    far_r,
    gather_s,
    gather_r,
):
    levels, T, C, block, m, R, F, tiles_all, bits, cuts = dims
    tiles_here = m * tiles_all // block
    tile = block // tiles_all
    N = T * C
    row = lax.axis_index("tm")
    col = lax.axis_index("col")
    me = row * C + col
    groups = F // ROWS
    G = groups * (R // LANES)
    parts = pieces(R)
    H = len(parts)
    last = levels - 1

    sources = (inv_hbm, low_hbm, up_hbm)

    def load(level, kind):
        return pltpu.make_async_copy(
            sources[kind].at[level, 0], raw.at[level, kind], in_sem.at[level, kind]
        )

    rhs_copy = pltpu.make_async_copy(rhs_hbm.at[0], rhs_v, rhs_sem.at[0])
    tip_c_copy = pltpu.make_async_copy(tip_c_hbm, tip_c, rhs_sem.at[1])
    tip_rhs_copy = pltpu.make_async_copy(tip_rhs_hbm, tip_rhs, rhs_sem.at[2])
    rhs_copy.start()
    load(0, 0).start()

    barrier = pltpu.get_barrier_semaphore()

    def greet(device):
        pl.semaphore_signal(barrier, inc=1, device_id=device, device_id_type=MESH)

    near = 2**bits * C
    each = G // near
    Q = T // 2**bits
    place = row // 2**bits
    seat = lax.rem(row, 2**bits) * C + col

    def over(count, action):
        @pl.loop(1, count)
        def _(k):
            action(k)

    def near_of(k):
        other = lax.rem(seat + k, near)
        return other, {"tm": place * 2**bits + other // C, "col": lax.rem(other, C)}

    def far_of(k):
        other = lax.rem(place + k, Q)
        return {"tm": other * 2**bits + lax.rem(row, 2**bits), "col": col}

    by_fours = bits == 2 and levels == 3

    def announce():
        if not by_fours:

            def anyone(k):
                other = lax.rem(me + k, N)
                greet({"tm": other // C, "col": lax.rem(other, C)})

            return over(N, anyone)
        over(near, lambda k: greet(near_of(k)[1]))
        over(Q, lambda k: greet(far_of(k)))
        inner = bit_of(0) != bit_of(1)

        @pl.when(inner)
        def _():
            beyond = lax.rem(row + 2 + (T - 4) * bit_of(0), T)
            greet({"tm": beyond, "col": col})

    def met():
        if not by_fours:
            return pl.semaphore_wait(barrier, N - 1)
        outer = 1 - lax.rem(bit_of(0) + bit_of(1), 2)
        pl.semaphore_wait(barrier, near - 1 + Q - 1 + outer)

    def bit_of(level):
        return lax.rem(row // 2**level, 2)

    announce()

    def split(level, kind):
        load(level, kind).wait()

        @pl.loop(0, tiles_all)
        def _(r):
            rows = pl.ds(pl.multiple_of(r * tile, tile), tile)
            for c in range(tiles_here):
                cols = pl.ds(c * tile, tile)
                w = raw[level, kind, rows, cols]
                if kind:
                    w = w * pattern[level, 0, kind - 1, c, r].astype(jnp.float32)
                high, low = halves_of(w)
                w_high[level, kind, rows, cols] = high
                w_low[level, kind, rows, cols] = low

    def rows_of(h):
        return pl.ds(parts[h][0], parts[h][1])

    def part_copy(level, h, k):
        return pltpu.make_async_remote_copy(
            src_ref=part.at[level, 0, rows_of(h)],
            dst_ref=part.at[level, k, rows_of(h)],
            send_sem=part_s.at[level, h, k - 1],
            recv_sem=part_r.at[level, h, k - 1],
            device_id={"tm": row, "col": lax.rem(col + k, C)},
            device_id_type=MESH,
        )

    def cuts_of(level):
        return 1 if level == last else cuts

    def span(level, q):
        width = m // cuts_of(level)
        return pl.ds(q * width, width)

    def row_copy(level, h, way, q):
        stride = 2**level
        at = (rows_of(h), span(level, q))
        if level == last:
            target = lax.rem(row + (T - stride if way == 0 else stride), T)
            source = send.at[(level, way, *at)]
        elif way == 0:
            target = lax.rem(row + T - 2 * stride + 4 * stride * bit_of(level), T)
            source = send.at[(level, bit_of(level), *at)]
        else:
            target = row + stride - 2 * stride * bit_of(level)
            source = joined.at[(level, *at)]
        return pltpu.make_async_remote_copy(
            src_ref=source,
            dst_ref=recv.at[(level, way, *at)],
            send_sem=row_s.at[level, h, way, q],
            recv_sem=row_r.at[level, h, way, q],
            device_id={"tm": target, "col": col},
            device_id_type=MESH,
        )

    def join(level, h, q):
        row_copy(level, h, 0, q).wait_recv()
        at = (rows_of(h), span(level, q))
        joined[(level, *at)] = (
            send[(level, 1 - bit_of(level), *at)] + recv[(level, 0, *at)]
        )
        row_copy(level, h, 1, q).start()

    def settled(level, h):
        for q in range(cuts_of(level)):
            row_copy(level, h, 1, q).wait_recv()
        value = cur[level, rows_of(h)] - recv[level, 1, rows_of(h)]
        if level == last:
            row_copy(level, h, 0, 0).wait_recv()
            value = value - recv[level, 0, rows_of(h)]
        return value

    def solve(level, h):
        if level:
            with scope(f"settle{level}{h}"):
                cur[level, rows_of(h)] = settled(level - 1, h)
        with scope(f"P{level}{h}"):
            high, low = halves_of(cur[level, rows_of(h)])
            stacked = jnp.concatenate([high, low], axis=0)
            part[level, 0, rows_of(h)] = product(
                stacked, high, w_high[level, 0], w_low[level, 0], NT
            )
            for k in range(1, C):
                part_copy(level, h, k).start()

    def add_tip(level, h, n):
        mine = pl.ds(pl.multiple_of(col * m, m), m)
        high, low = stk[0:n, mine], stk[n : 2 * n, mine]
        t_high, t_low = halves_of(tip_c[level, 0])
        dot = functools.partial(
            lax.dot_general, dimension_numbers=NT, preferred_element_type=jnp.float32
        )
        value = dot(t_high, high) + dot(t_high, low) + dot(t_low, high)
        start = parts[h][0]
        done = 0
        while done < n:
            b, lane = (start + done) // LANES, (start + done) % LANES
            w = min(LANES - lane, n - done)
            piece = value[:, done : done + w].reshape(groups, ROWS, w)
            at = (pl.ds(b * groups, groups), slice(None), pl.ds(lane, w))
            if level == 0:
                tip_acc[at] = piece
            else:
                tip_acc[at] = tip_acc[at] + piece
            done += w

    def spread(level, h):
        n = parts[h][1]
        with scope(f"xwait{level}{h}"):
            for k in range(1, C):
                part_copy(level, h, k).wait_recv()
        with scope(f"S{level}{h}"):
            total = part[level, 0, rows_of(h)]
            for k in range(1, C):
                total = total + part[level, k, rows_of(h)]
            high, low = halves_of(total)
            stk[0:n] = high
            stk[n : 2 * n] = low
        if level < last:
            ways = (bit_of(level), 1 - bit_of(level))
        else:
            ways = (0, 1)
        if level == last:
            with scope(f"tip{level}{h}"):
                add_tip(level, h, n)
                if h == H - 1:
                    tip_scatter()
        for i in range(2):
            for q in range(cuts_of(level)):
                with scope(f"DU{level}{h}"):
                    at = span(level, q)
                    send[level, ways[i], rows_of(h), at] = product(
                        stk[0 : 2 * n],
                        stk[0:n],
                        w_high[level, 1 + ways[i], :, at],
                        w_low[level, 1 + ways[i], :, at],
                        NN,
                    )
                    if level == last and h == H - 1:
                        continue
                    if i == 0 or level == last:
                        row_copy(level, h, i, q).start()
        if level < last:
            with scope(f"tip{level}{h}"):
                add_tip(level, h, n)

    def scatter_copy(k):
        other, device = near_of(k)
        return pltpu.make_async_remote_copy(
            src_ref=tip_acc.at[pl.ds(other * each, each)],
            dst_ref=tip_near.at[k - 1],
            send_sem=near_s.at[k - 1],
            recv_sem=near_r.at[k - 1],
            device_id=device,
            device_id_type=MESH,
        )

    def far_copy(k, here=True):
        slot = place if here else lax.rem(place + Q - k, Q)
        return pltpu.make_async_remote_copy(
            src_ref=tip_far.at[slot],
            dst_ref=tip_far.at[slot],
            send_sem=far_s.at[k - 1],
            recv_sem=far_r.at[k - 1],
            device_id=far_of(k),
            device_id_type=MESH,
        )

    def gather_copy(k, here=True):
        slot = seat if here else lax.rem(seat + near - k, near)
        return pltpu.make_async_remote_copy(
            src_ref=tip_all.at[pl.ds(slot * each, each)],
            dst_ref=tip_all.at[pl.ds(slot * each, each)],
            send_sem=gather_s.at[k - 1],
            recv_sem=gather_r.at[k - 1],
            device_id=near_of(k)[1],
            device_id_type=MESH,
        )

    def tip_scatter():
        over(near, lambda k: scatter_copy(k).start())

    def tip_reduce():
        over(near, lambda k: scatter_copy(k).wait_recv())
        tip_far[place] = tip_acc[pl.ds(seat * each, each)] + jnp.sum(
            tip_near[...], axis=0
        )
        over(Q, lambda k: far_copy(k).start())

    def tip_total():
        over(Q, lambda k: far_copy(k, False).wait_recv())
        tip_all[pl.ds(seat * each, each)] = jnp.sum(tip_far[...], axis=0)
        over(near, lambda k: gather_copy(k).start())

    def tip_finish():
        over(near, lambda k: gather_copy(k, False).wait_recv())
        tip_rhs_copy.wait()
        for b in range(R // LANES):
            lanes = slice(b * LANES, (b + 1) * LANES)
            total = tip_all[b * groups : (b + 1) * groups].reshape(F, LANES)
            tip_out[:, lanes] = tip_rhs[:, lanes] - total

    def final(h):
        start, n = parts[h]
        out[0, :, start : start + n] = settled(last, h).T

    with scope("rhs"):
        rhs_copy.wait()
        for kind in (1, 2):
            load(0, kind).start()
        cur[0] = rhs_v[...].T
    with scope("split00"):
        split(0, 0)
    tip_c_copy.start()
    tip_rhs_copy.start()
    with scope("barrier"):
        met()
    solve(0, 0)
    for kind in (1, 2):
        with scope("split0"):
            split(0, kind)
    for level in range(1, levels):
        for kind in range(3):
            load(level, kind).start()
    tip_c_copy.wait()

    def splits(level, *kinds):
        for kind in kinds:
            with scope(f"split{level}{kind}"):
                split(level, kind)

    def joins(q, level, h):
        if q < cuts_of(level):
            with scope(f"join{level}{h}"):
                join(level, h, q)

    def finals(h):
        with scope(f"final{h}"):
            final(h)

    actions = {
        "P": solve,
        "S": spread,
        "J": functools.partial(joins, 0),
        "K": functools.partial(joins, 1),
        "W": splits,
    }
    for step in ORDER:
        actions[step[0]](int(step[1]), int(step[2]))
    with scope("tipreduce"):
        tip_reduce()
    for i in range(2):
        row_copy(last, H - 1, i, 0).start()
    for h in range(H - 2):
        finals(h)
    with scope("tiptotal"):
        tip_total()
    finals(H - 2)
    with scope("tipfinish"):
        tip_finish()
    finals(H - 1)

    with scope("drain"):
        for level in range(levels):
            for h in range(H):
                for k in range(1, C):
                    part_copy(level, h, k).wait_send()
                for way in range(2):
                    for q in range(cuts_of(level)):
                        row_copy(level, h, way, q).wait_send()
        over(near, lambda k: scatter_copy(k).wait_send())
        over(Q, lambda k: far_copy(k).wait_send())
        over(near, lambda k: gather_copy(k).wait_send())


def solution(mesh):
    T, C = mesh.shape["tm"], mesh.shape["col"]

    def local(rhs, inverse, lower, upper, tile_pattern, tip_coupling, tip_rhs):
        levels, _, block, m = inverse.shape
        R = rhs.shape[2]
        F = tip_rhs.shape[0]
        G = (F // ROWS) * (R // LANES)
        cuts = 2 if m % (2 * LANES) == 0 else 1
        bits = 0
        while bits < 2 and G % (2 ** (bits + 1) * C) == 0 and T % 2 ** (bits + 1) == 0:
            bits += 1
        dims = (levels, T, C, block, m, R, F, tile_pattern.shape[3], bits, cuts)
        H = len(pieces(R))
        widest = max(n for _, n in pieces(R))
        Q = T // 2**bits
        f32, b16 = jnp.float32, jnp.bfloat16
        dma = pltpu.SemaphoreType.DMA
        peers = max(C - 1, 1)
        near = 2**bits * C
        anywhere = pl.BlockSpec(memory_space=pl.ANY)
        vmem = pl.BlockSpec(memory_space=pltpu.VMEM)
        return pl.pallas_call(
            functools.partial(kernel, dims),
            out_shape=(
                pltpu.VMEM((1, m, R), f32),
                pltpu.VMEM((F, R), f32),
            ),
            in_specs=[anywhere] * 4
            + [pl.BlockSpec(memory_space=pltpu.SMEM), anywhere, anywhere],
            out_specs=(vmem, vmem),
            scratch_shapes=[
                pltpu.VMEM((m, R), f32),
                pltpu.VMEM((levels, 1, F, m), f32),
                pltpu.VMEM((F, R), f32),
                pltpu.VMEM((levels, 3, block, m), f32),
                pltpu.VMEM((levels, 3, block, m), b16),
                pltpu.VMEM((levels, 3, block, m), b16),
                pltpu.VMEM((levels, R, m), f32),
                pltpu.VMEM((levels, C, R, block), f32),
                pltpu.VMEM((2 * widest, block), b16),
                pltpu.VMEM((levels, 2, R, m), f32),
                pltpu.VMEM((levels, 2, R, m), f32),
                pltpu.VMEM((max(levels - 1, 1), R, m), f32),
                pltpu.VMEM((G, ROWS, LANES), f32),
                pltpu.VMEM((near - 1, G // near, ROWS, LANES), f32),
                pltpu.VMEM((Q, G // near, ROWS, LANES), f32),
                pltpu.VMEM((G, ROWS, LANES), f32),
                dma((levels, 3)),
                dma((3,)),
                dma((levels, H, peers)),
                dma((levels, H, peers)),
                dma((levels, H, 2, cuts)),
                dma((levels, H, 2, cuts)),
                dma((near - 1,)),
                dma((near - 1,)),
                dma((Q - 1,)),
                dma((Q - 1,)),
                dma((near - 1,)),
                dma((near - 1,)),
            ],
            compiler_params=pltpu.CompilerParams(
                collective_id=0, has_side_effects=True, vmem_limit_bytes=63 * 2**20
            ),
        )(
            rhs,
            inverse,
            lower,
            upper,
            jnp.swapaxes(tile_pattern, 3, 4),
            tip_coupling,
            tip_rhs,
        )

    return jax.shard_map(
        local,
        mesh=mesh,
        in_specs=(
            P("tm", "col", None),
            P(None, "tm", None, "col"),
            P(None, "tm", None, "col"),
            P(None, "tm", None, "col"),
            P(None, "tm", None, None, "col"),
            P(None, "tm", None, "col"),
            P(),
        ),
        out_specs=(P("tm", "col", None), P()),
        check_vma=False,
    )
```

```python
import contextlib
import functools

import jax
import jax.numpy as jnp
from jax import lax
from jax.experimental import pallas as pl
from jax.experimental.pallas import tpu as pltpu
from jax.sharding import PartitionSpec as P

MESH = pl.DeviceIdType.MESH
LANES = 128
ROWS = 8
TRACE = False
NT = (((1,), (1,)), ((), ()))
NN = (((1,), (0,)), ((), ()))


def scope(name):
    return jax.named_scope(name) if TRACE else contextlib.nullcontext()


def halves_of(x):
    high = x.astype(jnp.bfloat16)
    low = (x - high.astype(jnp.float32)).astype(jnp.bfloat16)
    return high, low


def product(stacked, high, w_high, w_low, form):
    rows = high.shape[0]
    dot = functools.partial(
        lax.dot_general, dimension_numbers=form, preferred_element_type=jnp.float32
    )
    both = dot(stacked, w_high)
    return both[:rows] + both[rows:] + dot(high, w_low)


ORDER = (
    "S00", "P01", "W10", "W11", "J00", "S01", "K00", "W12", "W20", "J01", "W21", "W22",
    "K01", "J02", "P10", "K02", "S10", "J03", "P11", "K03", "S11", "P12", "J10", "S12",
    "K10", "P13", "J11", "S13", "P20", "J12", "S20", "P21", "J13", "S21", "T04", "P22",
    "S22", "T14", "P23", "T23", "S23",
)
PIECES = 4
QUARTERS = 4
PAIRED = (0,)
DIRECT = ()
HALVED = ((0, 0), (0, 1), (0, 2), (0, 3), (1, 0))


def pieces(R):
    return tuple((R * h // PIECES, R // PIECES) for h in range(PIECES))


def kernel(
    dims,
    rhs_hbm,
    inv_hbm,
    low_hbm,
    up_hbm,
    pattern_hbm,
    tip_c_hbm,
    tip_rhs_hbm,
    out,
    tip_out,
    pattern,
    rhs_v,
    tip_c,
    tip_rhs,
    raw,
    w_high,
    w_low,
    cur,
    part,
    s_high,
    s_low,
    send,
    recv,
    joined,
    tip_acc,
    tip_near,
    tip_far,
    tip_all,
    in_sem,
    rhs_sem,
    first_sem,
    part_r,
    join_r,
    row_r,
    tip_r,
    sent,
):
    levels, T, C, block, m, R, F, tiles_all, bits, cuts = dims
    tiles_here = m * tiles_all // block
    tile = block // tiles_all
    N = T * C
    row = lax.axis_index("tm")
    col = lax.axis_index("col")
    me = row * C + col
    groups = F // ROWS
    G = groups * (R // LANES)
    parts = pieces(R)
    H = len(parts)
    last = levels - 1

    sources = (inv_hbm, low_hbm, up_hbm)

    def load(level, kind):
        return pltpu.make_async_copy(
            sources[kind].at[level, 0], raw.at[level, kind], in_sem.at[level, kind]
        )

    def first_load(q):
        rows = pl.ds(q * (block // QUARTERS), block // QUARTERS)
        return pltpu.make_async_copy(
            inv_hbm.at[0, 0, rows], raw.at[0, 0, rows], first_sem.at[q]
        )

    rhs_copy = pltpu.make_async_copy(rhs_hbm.at[0], rhs_v, rhs_sem.at[0])
    pattern_copy = pltpu.make_async_copy(pattern_hbm, pattern, rhs_sem.at[3])
    tip_c_copy = pltpu.make_async_copy(tip_c_hbm, tip_c, rhs_sem.at[1])
    tip_rhs_copy = pltpu.make_async_copy(tip_rhs_hbm, tip_rhs, rhs_sem.at[2])
    rhs_copy.start()
    for q in range(QUARTERS):
        first_load(q).start()
    pattern_copy.start()

    barrier = pltpu.get_barrier_semaphore()

    def greet(device):
        pl.semaphore_signal(barrier, inc=1, device_id=device, device_id_type=MESH)

    near = 2**bits * C
    each = G // near
    Q = T // 2**bits
    place = row // 2**bits
    seat = lax.rem(row, 2**bits) * C + col

    def over(count, action):
        @pl.loop(1, count)
        def _(k):
            action(k)

    def near_of(k):
        other = lax.rem(seat + k, near)
        return other, {"tm": place * 2**bits + other // C, "col": lax.rem(other, C)}

    def far_of(k):
        other = lax.rem(place + k, Q)
        return {"tm": other * 2**bits + lax.rem(row, 2**bits), "col": col}

    by_fours = bits == 2 and levels == 3

    def announce():
        if not by_fours:

            def anyone(k):
                other = lax.rem(me + k, N)
                greet({"tm": other // C, "col": lax.rem(other, C)})

            return over(N, anyone)
        over(near, lambda k: greet(near_of(k)[1]))
        over(Q, lambda k: greet(far_of(k)))
        greet({"tm": lax.rem(row + T - 2 + 4 * bit_of(1), T), "col": col})

        @pl.when(bit_of(0) == bit_of(1))
        def _():
            greet({"tm": lax.rem(row + T - 1 + 2 * bit_of(1), T), "col": col})

    def met():
        if not by_fours:
            return pl.semaphore_wait(barrier, N - 1)
        outer = 1 - lax.rem(bit_of(0) + bit_of(1), 2)
        pl.semaphore_wait(barrier, near + Q - 1 + outer)

    def bit_of(level):
        return lax.rem(row // 2**level, 2)

    announce()

    def split(level, kind):
        if level or kind:
            load(level, kind).wait()
            return split_tiles(level, kind, 0, tiles_all)
        for q in range(QUARTERS):
            first_load(q).wait()
            split_tiles(0, 0, tiles_all * q // QUARTERS, tiles_all * (q + 1) // QUARTERS)

    def split_tiles(level, kind, begin, end):
        @pl.loop(begin, end)
        def _(r):
            rows = pl.ds(pl.multiple_of(r * tile, tile), tile)
            for c in range(tiles_here):
                cols = pl.ds(c * tile, tile)
                w = raw[level, kind, rows, cols]
                if kind:
                    w = w * pattern[level, 0, kind - 1, c, r].astype(jnp.float32)
                high, low = halves_of(w)
                w_high[level, kind, rows, cols] = high
                w_low[level, kind, rows, cols] = low

    def all_of(ref, sem):
        pltpu.make_async_copy(ref, ref, sem).wait()

    def rows_of(h):
        return pl.ds(parts[h][0], parts[h][1])

    def group(level, g):
        width = 2 if level in PAIRED else 1
        return range(g * width, (g + 1) * width)

    def groups_of(level):
        return H // 2 if level in PAIRED else H

    def rows_in(level, g):
        members = group(level, g)
        start = parts[members[0]][0]
        return pl.ds(start, parts[members[-1]][0] + parts[members[-1]][1] - start)

    def part_copy(level, g, k):
        return pltpu.make_async_remote_copy(
            src_ref=part.at[level, 0, rows_in(level, g)],
            dst_ref=part.at[level, k, rows_in(level, g)],
            send_sem=sent.at[0],
            recv_sem=part_r.at[level, g, k - 1],
            device_id={"tm": row, "col": lax.rem(col + k, C)},
            device_id_type=MESH,
        )

    def direct(level, h):
        return level == last or (level, h) in DIRECT

    def cuts_of(level, h):
        return cuts if (level, h) in HALVED and not direct(level, h) else 1

    def span(level, h, q):
        width = m // cuts_of(level, h)
        return pl.ds(q * width, width)

    def row_copy(level, h, way, q):
        stride = 2**level
        at = (rows_of(h), span(level, h, q))
        arrival = row_r.at[level, h]
        if direct(level, h):
            target = lax.rem(row + (T - stride if way == 0 else stride), T)
            source = send.at[(level, way, *at)]
        elif way == 0:
            target = lax.rem(row + T - 2 * stride + 4 * stride * bit_of(level), T)
            source = send.at[(level, bit_of(level), *at)]
            arrival = join_r.at[level, h, q]
        else:
            target = row + stride - 2 * stride * bit_of(level)
            source = joined.at[(level, *at)]
        return pltpu.make_async_remote_copy(
            src_ref=source,
            dst_ref=recv.at[(level, way, *at)],
            send_sem=sent.at[1],
            recv_sem=arrival,
            device_id={"tm": target, "col": col},
            device_id_type=MESH,
        )

    def join(level, h, q):
        row_copy(level, h, 0, q).wait_recv()
        at = (rows_of(h), span(level, h, q))
        joined[(level, *at)] = (
            send[(level, 1 - bit_of(level), *at)] + recv[(level, 0, *at)]
        )
        row_copy(level, h, 1, q).start()

    def settled(level, h):
        ways = pl.ds(0, 2) if direct(level, h) else pl.ds(1, 1)
        all_of(recv.at[level, ways, rows_of(h)], row_r.at[level, h])
        value = cur[level, rows_of(h)] - recv[level, 1, rows_of(h)]
        if direct(level, h):
            value = value - recv[level, 0, rows_of(h)]
        return value

    def solve(level, g):
        if level:
            for h in group(level, g):
                with scope(f"settle{level}{h}"):
                    cur[level, rows_of(h)] = settled(level - 1, h)
        with scope(f"P{level}{g}"):
            rows = rows_in(level, g)
            high, low = halves_of(cur[level, rows])
            stacked = jnp.concatenate([high, low], axis=0)
            part[level, 0, rows] = product(
                stacked, high, w_high[level, 0], w_low[level, 0], NT
            )
            for k in range(1, C):
                part_copy(level, g, k).start()

    def add_tip(level, first, end):
        start = parts[first][0]
        n = parts[end - 1][0] + parts[end - 1][1] - start
        mine = pl.ds(pl.multiple_of(col * m, m), m)
        high = s_high[level, pl.ds(start, n), mine]
        low = s_low[level, pl.ds(start, n), mine]
        t_high, t_low = halves_of(tip_c[level, 0])
        dot = functools.partial(
            lax.dot_general, dimension_numbers=NT, preferred_element_type=jnp.float32
        )
        value = dot(t_high, high) + dot(t_high, low) + dot(t_low, high)
        done = 0
        while done < n:
            b, lane = (start + done) // LANES, (start + done) % LANES
            w = min(LANES - lane, n - done)
            piece = value[:, done : done + w].reshape(groups, ROWS, w)
            at = (pl.ds(b * groups, groups), slice(None), pl.ds(lane, w))
            if level == 0:
                tip_acc[at] = piece
            else:
                tip_acc[at] = tip_acc[at] + piece
            done += w

    def spread(level, g):
        rows = rows_in(level, g)
        members = group(level, g)
        closing = level == last and members[-1] == H - 1
        with scope(f"xwait{level}{g}"):
            for k in range(1, C):
                part_copy(level, g, k).wait_recv()
        with scope(f"S{level}{g}"):
            total = part[level, 0, rows]
            for k in range(1, C):
                total = total + part[level, k, rows]
            high, low = halves_of(total)
            s_high[level, rows] = high
            s_low[level, rows] = low
        straight = direct(level, members[0])
        ways = (0, 1) if straight else (bit_of(level), 1 - bit_of(level))
        if closing:
            with scope(f"tip{level}{g}"):
                add_tip(level, members[0], H)
                tip_scatter()
        for i in range(2):
            with scope(f"DU{level}{g}"):
                high = s_high[level, rows]
                stacked = jnp.concatenate([high, s_low[level, rows]], axis=0)
                send[level, ways[i], rows] = product(
                    stacked,
                    high,
                    w_high[level, 1 + ways[i]],
                    w_low[level, 1 + ways[i]],
                    NN,
                )
                if not closing and (i == 0 or straight):
                    for h in members:
                        for q in range(cuts_of(level, h)):
                            row_copy(level, h, i, q).start()

    def scatter_copy(k):
        other, device = near_of(k)
        return pltpu.make_async_remote_copy(
            src_ref=tip_acc.at[pl.ds(other * each, each)],
            dst_ref=tip_near.at[k - 1],
            send_sem=sent.at[2],
            recv_sem=tip_r.at[0],
            device_id=device,
            device_id_type=MESH,
        )

    def far_copy(k):
        return pltpu.make_async_remote_copy(
            src_ref=tip_far.at[place],
            dst_ref=tip_far.at[place],
            send_sem=sent.at[3],
            recv_sem=tip_r.at[1],
            device_id=far_of(k),
            device_id_type=MESH,
        )

    def gather_copy(k):
        mine = pl.ds(seat * each, each)
        return pltpu.make_async_remote_copy(
            src_ref=tip_all.at[mine],
            dst_ref=tip_all.at[mine],
            send_sem=sent.at[4],
            recv_sem=tip_r.at[2],
            device_id=near_of(k)[1],
            device_id_type=MESH,
        )

    def tip_scatter():
        over(near, lambda k: scatter_copy(k).start())

    def tip_reduce():
        all_of(tip_near, tip_r.at[0])
        tip_far[place] = tip_acc[pl.ds(seat * each, each)] + jnp.sum(
            tip_near[...], axis=0
        )
        over(Q, lambda k: far_copy(k).start())

    def tip_total():
        all_of(tip_far.at[pl.ds(1, Q - 1)], tip_r.at[1])
        tip_all[pl.ds(seat * each, each)] = jnp.sum(tip_far[...], axis=0)
        over(near, lambda k: gather_copy(k).start())

    def tip_finish():
        all_of(tip_near, tip_r.at[2])
        tip_rhs_copy.wait()
        for b in range(R // LANES):
            lanes = slice(b * LANES, (b + 1) * LANES)
            total = tip_all[b * groups : (b + 1) * groups].reshape(F, LANES)
            tip_out[:, lanes] = tip_rhs[:, lanes] - total

    def final(h):
        start, n = parts[h]
        out[0, :, start : start + n] = settled(last, h).T

    with scope("rhs"):
        rhs_copy.wait()
        for kind in (1, 2):
            load(0, kind).start()
        cur[0] = rhs_v[...].T
    with scope("split00"):
        split(0, 0)
    tip_c_copy.start()
    tip_rhs_copy.start()
    with scope("barrier"):
        met()
    solve(0, 0)
    pattern_copy.wait()
    for kind in (1, 2):
        with scope("split0"):
            split(0, kind)
    for level in range(1, levels):
        for kind in range(3):
            load(level, kind).start()
    tip_c_copy.wait()

    def splits(level, *kinds):
        for kind in kinds:
            with scope(f"split{level}{kind}"):
                split(level, kind)

    def joins(q, level, h):
        if q < cuts_of(level, h) and not direct(level, h):
            with scope(f"join{level}{h}"):
                join(level, h, q)

    def tips(level, end):
        with scope(f"tip{level}{end}"):
            add_tip(level, 0, end)

    def finals(h):
        with scope(f"final{h}"):
            final(h)

    actions = {
        "P": solve,
        "S": spread,
        "J": functools.partial(joins, 0),
        "K": functools.partial(joins, 1),
        "W": splits,
        "T": tips,
    }
    for step in ORDER:
        actions[step[0]](int(step[1]), int(step[2]))
    with scope("tipreduce"):
        tip_reduce()
    for i in range(2):
        row_copy(last, H - 1, i, 0).start()
    for h in range(H - 2):
        finals(h)
    with scope("tiptotal"):
        tip_total()
    finals(H - 2)
    with scope("tipfinish"):
        tip_finish()
    finals(H - 1)

    with scope("drain"):
        if C > 1:
            all_of(part.at[:, pl.ds(1, C - 1)], sent.at[0])
        all_of(recv, sent.at[1])
        all_of(tip_near, sent.at[2])
        all_of(tip_far.at[pl.ds(1, Q - 1)], sent.at[3])
        all_of(tip_near, sent.at[4])


def solution(mesh):
    T, C = mesh.shape["tm"], mesh.shape["col"]

    def local(rhs, inverse, lower, upper, tile_pattern, tip_coupling, tip_rhs):
        levels, _, block, m = inverse.shape
        R = rhs.shape[2]
        F = tip_rhs.shape[0]
        G = (F // ROWS) * (R // LANES)
        cuts = 2 if m % (2 * LANES) == 0 else 1
        bits = 0
        while bits < 2 and G % (2 ** (bits + 1) * C) == 0 and T % 2 ** (bits + 1) == 0:
            bits += 1
        dims = (levels, T, C, block, m, R, F, tile_pattern.shape[3], bits, cuts)
        H = len(pieces(R))
        tiles_all, tiles_here = tile_pattern.shape[3:]
        Q = T // 2**bits
        f32, b16 = jnp.float32, jnp.bfloat16
        dma = pltpu.SemaphoreType.DMA
        peers = max(C - 1, 1)
        near = 2**bits * C
        anywhere = pl.BlockSpec(memory_space=pl.ANY)
        vmem = pl.BlockSpec(memory_space=pltpu.VMEM)
        return pl.pallas_call(
            functools.partial(kernel, dims),
            out_shape=(
                pltpu.VMEM((1, m, R), f32),
                pltpu.VMEM((F, R), f32),
            ),
            in_specs=[anywhere] * 4
            + [anywhere] * 3,
            out_specs=(vmem, vmem),
            scratch_shapes=[
                pltpu.SMEM((levels, 1, 2, tiles_here, tiles_all), jnp.int32),
                pltpu.VMEM((m, R), f32),
                pltpu.VMEM((levels, 1, F, m), f32),
                pltpu.VMEM((F, R), f32),
                pltpu.VMEM((levels, 3, block, m), f32),
                pltpu.VMEM((levels, 3, block, m), b16),
                pltpu.VMEM((levels, 3, block, m), b16),
                pltpu.VMEM((levels, R, m), f32),
                pltpu.VMEM((levels, C, R, block), f32),
                pltpu.VMEM((levels, R, block), b16),
                pltpu.VMEM((levels, R, block), b16),
                pltpu.VMEM((levels, 2, R, m), f32),
                pltpu.VMEM((levels, 2, R, m), f32),
                pltpu.VMEM((max(levels - 1, 1), R, m), f32),
                pltpu.VMEM((G, ROWS, LANES), f32),
                pltpu.VMEM((near - 1, G // near, ROWS, LANES), f32),
                pltpu.VMEM((Q, G // near, ROWS, LANES), f32),
                pltpu.VMEM((G, ROWS, LANES), f32),
                dma((levels, 3)),
                dma((4,)),
                dma((QUARTERS,)),
                dma((levels, H, peers)),
                dma((max(levels - 1, 1), H, cuts)),
                dma((levels, H)),
                dma((3,)),
                dma((5,)),
            ],
            compiler_params=pltpu.CompilerParams(
                collective_id=0, has_side_effects=True, vmem_limit_bytes=63 * 2**20
            ),
        )(
            rhs,
            inverse,
            lower,
            upper,
            jnp.swapaxes(tile_pattern, 3, 4),
            tip_coupling,
            tip_rhs,
        )

    return jax.shard_map(
        local,
        mesh=mesh,
        in_specs=(
            P("tm", "col", None),
            P(None, "tm", None, "col"),
            P(None, "tm", None, "col"),
            P(None, "tm", None, "col"),
            P(None, "tm", None, None, "col"),
            P(None, "tm", None, "col"),
            P(),
        ),
        out_specs=(P("tm", "col", None), P()),
        check_vma=False,
    )
```

```python
import contextlib
import functools

import jax
import jax.numpy as jnp
from jax import lax
from jax.experimental import pallas as pl
from jax.experimental.pallas import tpu as pltpu
from jax.sharding import PartitionSpec as P

MESH = pl.DeviceIdType.MESH
LANES = 128
ROWS = 8
TRACE = False
NT = (((1,), (1,)), ((), ()))
NN = (((1,), (0,)), ((), ()))


def scope(name):
    return jax.named_scope(name) if TRACE else contextlib.nullcontext()


def halves_of(x):
    high = x.astype(jnp.bfloat16)
    low = (x - high.astype(jnp.float32)).astype(jnp.bfloat16)
    return high, low


def product(stacked, high, w_high, w_low, form):
    rows = high.shape[0]
    dot = functools.partial(
        lax.dot_general, dimension_numbers=form, preferred_element_type=jnp.float32
    )
    both = dot(stacked, w_high)
    return both[:rows] + both[rows:] + dot(high, w_low)


ORDER = (
    "S00", "P01", "W10", "W11", "J00", "S01", "K00", "W12", "W20", "J01", "W21", "W22",
    "K01", "J02", "P10", "K02", "S10", "J03", "P11", "K03", "S11", "P12", "J10", "S12",
    "K10", "P13", "J11", "S13", "P20", "J12", "S20", "P21", "J13", "S21", "T04", "P22",
    "S22", "T14", "P23", "T23", "S23",
)
SIXTEENTHS = (4, 8, 12, 16)
QUARTERS = 4
PAIRED = (0,)
DIRECT = ()
HALVED = ((0, 0), (0, 1), (0, 2), (0, 3), (1, 0))


def pieces(R):
    ends = [R * e // SIXTEENTHS[-1] for e in SIXTEENTHS]
    return tuple((a, b - a) for a, b in zip([0] + ends, ends))


def kernel(
    dims,
    rhs_hbm,
    inv_hbm,
    low_hbm,
    up_hbm,
    pattern_hbm,
    tip_c_hbm,
    tip_rhs_hbm,
    out,
    tip_out,
    pattern,
    rhs_v,
    tip_c,
    tip_rhs,
    raw,
    w_high,
    w_low,
    cur,
    part,
    s_high,
    s_low,
    send,
    recv,
    joined,
    tip_acc,
    tip_near,
    tip_far,
    tip_all,
    in_sem,
    rhs_sem,
    first_sem,
    part_r,
    join_r,
    row_r,
    tip_r,
    sent,
):
    levels, T, C, block, m, R, F, tiles_all, bits, cuts = dims
    tiles_here = m * tiles_all // block
    tile = block // tiles_all
    N = T * C
    row = lax.axis_index("tm")
    col = lax.axis_index("col")
    me = row * C + col
    groups = F // ROWS
    G = groups * (R // LANES)
    parts = pieces(R)
    H = len(parts)
    last = levels - 1

    sources = (inv_hbm, low_hbm, up_hbm)

    def load(level, kind):
        return pltpu.make_async_copy(
            sources[kind].at[level, 0], raw.at[level, kind], in_sem.at[level, kind]
        )

    def first_load(q):
        rows = pl.ds(q * (block // QUARTERS), block // QUARTERS)
        return pltpu.make_async_copy(
            inv_hbm.at[0, 0, rows], raw.at[0, 0, rows], first_sem.at[q]
        )

    rhs_copy = pltpu.make_async_copy(rhs_hbm.at[0], rhs_v, rhs_sem.at[0])
    pattern_copy = pltpu.make_async_copy(pattern_hbm, pattern, rhs_sem.at[3])
    tip_c_copy = pltpu.make_async_copy(tip_c_hbm, tip_c, rhs_sem.at[1])
    tip_rhs_copy = pltpu.make_async_copy(tip_rhs_hbm, tip_rhs, rhs_sem.at[2])
    rhs_copy.start()
    for q in range(QUARTERS):
        first_load(q).start()
    pattern_copy.start()

    barrier = pltpu.get_barrier_semaphore()

    def greet(device):
        pl.semaphore_signal(barrier, inc=1, device_id=device, device_id_type=MESH)

    near = 2**bits * C
    each = G // near
    Q = T // 2**bits
    place = row // 2**bits
    seat = lax.rem(row, 2**bits) * C + col

    def over(count, action):
        @pl.loop(1, count)
        def _(k):
            action(k)

    def near_of(k):
        other = lax.rem(seat + k, near)
        return other, {"tm": place * 2**bits + other // C, "col": lax.rem(other, C)}

    def far_of(k):
        other = lax.rem(place + k, Q)
        return {"tm": other * 2**bits + lax.rem(row, 2**bits), "col": col}

    by_fours = bits == 2 and levels == 3

    def announce():
        if not by_fours:

            def anyone(k):
                other = lax.rem(me + k, N)
                greet({"tm": other // C, "col": lax.rem(other, C)})

            return over(N, anyone)
        over(near, lambda k: greet(near_of(k)[1]))
        over(Q, lambda k: greet(far_of(k)))
        greet({"tm": lax.rem(row + T - 2 + 4 * bit_of(1), T), "col": col})

        @pl.when(bit_of(0) == bit_of(1))
        def _():
            greet({"tm": lax.rem(row + T - 1 + 2 * bit_of(1), T), "col": col})

    def met():
        if not by_fours:
            return pl.semaphore_wait(barrier, N - 1)
        outer = 1 - lax.rem(bit_of(0) + bit_of(1), 2)
        pl.semaphore_wait(barrier, near + Q - 1 + outer)

    def bit_of(level):
        return lax.rem(row // 2**level, 2)

    announce()

    def split(level, kind):
        if level or kind:
            load(level, kind).wait()
            return split_tiles(level, kind, 0, tiles_all)
        for q in range(QUARTERS):
            first_load(q).wait()
            split_tiles(0, 0, tiles_all * q // QUARTERS, tiles_all * (q + 1) // QUARTERS)

    def split_tiles(level, kind, begin, end):
        @pl.loop(begin, end)
        def _(r):
            rows = pl.ds(pl.multiple_of(r * tile, tile), tile)
            for c in range(tiles_here):
                cols = pl.ds(c * tile, tile)
                w = raw[level, kind, rows, cols]
                if kind:
                    w = w * pattern[level, 0, kind - 1, c, r].astype(jnp.float32)
                high, low = halves_of(w)
                w_high[level, kind, rows, cols] = high
                w_low[level, kind, rows, cols] = low

    def all_of(ref, sem):
        pltpu.make_async_copy(ref, ref, sem).wait()

    def rows_of(h):
        return pl.ds(parts[h][0], parts[h][1])

    def group(level, g):
        width = 2 if level in PAIRED else 1
        return range(g * width, (g + 1) * width)

    def groups_of(level):
        return H // 2 if level in PAIRED else H

    def rows_in(level, g):
        members = group(level, g)
        start = parts[members[0]][0]
        return pl.ds(start, parts[members[-1]][0] + parts[members[-1]][1] - start)

    def part_copy(level, g, k):
        return pltpu.make_async_remote_copy(
            src_ref=part.at[level, 0, rows_in(level, g)],
            dst_ref=part.at[level, k, rows_in(level, g)],
            send_sem=sent.at[0],
            recv_sem=part_r.at[level, g, k - 1],
            device_id={"tm": row, "col": lax.rem(col + k, C)},
            device_id_type=MESH,
        )

    def direct(level, h):
        return level == last or (level, h) in DIRECT

    def cuts_of(level, h):
        return cuts if (level, h) in HALVED and not direct(level, h) else 1

    def span(level, h, q):
        width = m // cuts_of(level, h)
        return pl.ds(q * width, width)

    def row_copy(level, h, way, q):
        stride = 2**level
        at = (rows_of(h), span(level, h, q))
        arrival = row_r.at[level, h]
        if direct(level, h):
            target = lax.rem(row + T - stride + 2 * stride * way, T)
            source = send.at[(level, way, *at)]
        elif isinstance(way, int) and way == 0:
            target = lax.rem(row + T - 2 * stride + 4 * stride * bit_of(level), T)
            source = send.at[(level, bit_of(level), *at)]
            arrival = join_r.at[level, h, q]
        else:
            target = row + stride - 2 * stride * bit_of(level)
            source = joined.at[(level, *at)]
        return pltpu.make_async_remote_copy(
            src_ref=source,
            dst_ref=recv.at[(level, way, *at)],
            send_sem=sent.at[1],
            recv_sem=arrival,
            device_id={"tm": target, "col": col},
            device_id_type=MESH,
        )

    def join(level, h, q):
        row_copy(level, h, 0, q).wait_recv()
        at = (rows_of(h), span(level, h, q))
        joined[(level, *at)] = (
            send[(level, 1 - bit_of(level), *at)] + recv[(level, 0, *at)]
        )
        row_copy(level, h, 1, q).start()

    def settled(level, h):
        ways = pl.ds(0, 2) if direct(level, h) else pl.ds(1, 1)
        all_of(recv.at[level, ways, rows_of(h)], row_r.at[level, h])
        value = cur[level, rows_of(h)] - recv[level, 1, rows_of(h)]
        if direct(level, h):
            value = value - recv[level, 0, rows_of(h)]
        return value

    def solve(level, g):
        if level:
            for h in group(level, g):
                with scope(f"settle{level}{h}"):
                    cur[level, rows_of(h)] = settled(level - 1, h)
        with scope(f"P{level}{g}"):
            rows = rows_in(level, g)
            high, low = halves_of(cur[level, rows])
            stacked = jnp.concatenate([high, low], axis=0)
            part[level, 0, rows] = product(
                stacked, high, w_high[level, 0], w_low[level, 0], NT
            )
            for k in range(1, C):
                part_copy(level, g, k).start()

    def add_tip(level, first, end):
        start = parts[first][0]
        n = parts[end - 1][0] + parts[end - 1][1] - start
        mine = pl.ds(pl.multiple_of(col * m, m), m)
        high = s_high[level, pl.ds(start, n), mine]
        low = s_low[level, pl.ds(start, n), mine]
        t_high, t_low = halves_of(tip_c[level, 0])
        dot = functools.partial(
            lax.dot_general, dimension_numbers=NT, preferred_element_type=jnp.float32
        )
        value = dot(t_high, high) + dot(t_high, low) + dot(t_low, high)
        done = 0
        while done < n:
            b, lane = (start + done) // LANES, (start + done) % LANES
            w = min(LANES - lane, n - done)
            piece = value[:, done : done + w].reshape(groups, ROWS, w)
            at = (pl.ds(b * groups, groups), slice(None), pl.ds(lane, w))
            if level == 0:
                tip_acc[at] = piece
            else:
                tip_acc[at] = tip_acc[at] + piece
            done += w

    def spread(level, g):
        rows = rows_in(level, g)
        members = group(level, g)
        closing = level == last and members[-1] == H - 1
        with scope(f"xwait{level}{g}"):
            for k in range(1, C):
                part_copy(level, g, k).wait_recv()
        with scope(f"S{level}{g}"):
            total = part[level, 0, rows]
            for k in range(1, C):
                total = total + part[level, k, rows]
            high, low = halves_of(total)
            s_high[level, rows] = high
            s_low[level, rows] = low
        straight = direct(level, members[0])
        over_end = (row + 2**level) // T
        ways = (over_end, 1 - over_end) if straight else (bit_of(level), 1 - bit_of(level))
        if closing:
            with scope(f"tip{level}{g}"):
                add_tip(level, members[0], H)
                tip_scatter()
        for i in range(2):
            with scope(f"DU{level}{g}"):
                high = s_high[level, rows]
                stacked = jnp.concatenate([high, s_low[level, rows]], axis=0)
                send[level, ways[i], rows] = product(
                    stacked,
                    high,
                    w_high[level, 1 + ways[i]],
                    w_low[level, 1 + ways[i]],
                    NN,
                )
                if not closing and (i == 0 or straight):
                    for h in members:
                        for q in range(cuts_of(level, h)):
                            row_copy(level, h, ways[i] if straight else i, q).start()

    def scatter_copy(k):
        other, device = near_of(k)
        return pltpu.make_async_remote_copy(
            src_ref=tip_acc.at[pl.ds(other * each, each)],
            dst_ref=tip_near.at[k - 1],
            send_sem=sent.at[2],
            recv_sem=tip_r.at[0],
            device_id=device,
            device_id_type=MESH,
        )

    def far_copy(k):
        return pltpu.make_async_remote_copy(
            src_ref=tip_far.at[place],
            dst_ref=tip_far.at[place],
            send_sem=sent.at[3],
            recv_sem=tip_r.at[1],
            device_id=far_of(k),
            device_id_type=MESH,
        )

    def gather_copy(k):
        mine = pl.ds(seat * each, each)
        return pltpu.make_async_remote_copy(
            src_ref=tip_all.at[mine],
            dst_ref=tip_all.at[mine],
            send_sem=sent.at[4],
            recv_sem=tip_r.at[2],
            device_id=near_of(k)[1],
            device_id_type=MESH,
        )

    def tip_scatter():
        over(near, lambda k: scatter_copy(k).start())

    def tip_reduce():
        all_of(tip_near, tip_r.at[0])
        tip_far[place] = tip_acc[pl.ds(seat * each, each)] + jnp.sum(
            tip_near[...], axis=0
        )
        over(Q, lambda k: far_copy(k).start())

    def tip_total():
        all_of(tip_far.at[pl.ds(1, Q - 1)], tip_r.at[1])
        tip_all[pl.ds(seat * each, each)] = jnp.sum(tip_far[...], axis=0)
        over(near, lambda k: gather_copy(k).start())

    def tip_finish():
        all_of(tip_near, tip_r.at[2])
        tip_rhs_copy.wait()
        for b in range(R // LANES):
            lanes = slice(b * LANES, (b + 1) * LANES)
            total = tip_all[b * groups : (b + 1) * groups].reshape(F, LANES)
            tip_out[:, lanes] = tip_rhs[:, lanes] - total

    def final(h):
        start, n = parts[h]
        out[0, :, start : start + n] = settled(last, h).T

    with scope("rhs"):
        rhs_copy.wait()
        for kind in (1, 2):
            load(0, kind).start()
        cur[0] = rhs_v[...].T
    with scope("split00"):
        split(0, 0)
    tip_c_copy.start()
    tip_rhs_copy.start()
    with scope("barrier"):
        met()
    solve(0, 0)
    pattern_copy.wait()
    for kind in (1, 2):
        with scope("split0"):
            split(0, kind)
    for level in range(1, levels):
        for kind in range(3):
            load(level, kind).start()
    tip_c_copy.wait()

    def splits(level, *kinds):
        for kind in kinds:
            with scope(f"split{level}{kind}"):
                split(level, kind)

    def joins(q, level, h):
        if q < cuts_of(level, h) and not direct(level, h):
            with scope(f"join{level}{h}"):
                join(level, h, q)

    def tips(level, end):
        with scope(f"tip{level}{end}"):
            add_tip(level, 0, end)

    def finals(h):
        with scope(f"final{h}"):
            final(h)

    actions = {
        "P": solve,
        "S": spread,
        "J": functools.partial(joins, 0),
        "K": functools.partial(joins, 1),
        "W": splits,
        "T": tips,
    }
    for step in ORDER:
        actions[step[0]](int(step[1]), int(step[2]))
    with scope("tipreduce"):
        tip_reduce()
    over_end = (row + 2**last) // T
    for way in (over_end, 1 - over_end):
        row_copy(last, H - 1, way, 0).start()
    for h in range(H - 2):
        finals(h)
    with scope("tiptotal"):
        tip_total()
    finals(H - 2)
    with scope("tipfinish"):
        tip_finish()
    finals(H - 1)

    with scope("drain"):
        if C > 1:
            all_of(part.at[:, pl.ds(1, C - 1)], sent.at[0])
        all_of(recv, sent.at[1])
        all_of(tip_near, sent.at[2])
        all_of(tip_far.at[pl.ds(1, Q - 1)], sent.at[3])
        all_of(tip_near, sent.at[4])


def store(main, tip, main_out, tip_out, sem):
    copies = [
        pltpu.make_async_copy(main, main_out, sem.at[0]),
        pltpu.make_async_copy(tip, tip_out, sem.at[1]),
    ]
    for copy in copies:
        copy.start()
    for copy in copies:
        copy.wait()


def solution(mesh):
    T, C = mesh.shape["tm"], mesh.shape["col"]

    def local(rhs, inverse, lower, upper, tile_pattern, tip_coupling, tip_rhs):
        levels, _, block, m = inverse.shape
        R = rhs.shape[2]
        F = tip_rhs.shape[0]
        G = (F // ROWS) * (R // LANES)
        cuts = 2 if m % (2 * LANES) == 0 else 1
        bits = 0
        while bits < 2 and G % (2 ** (bits + 1) * C) == 0 and T % 2 ** (bits + 1) == 0:
            bits += 1
        dims = (levels, T, C, block, m, R, F, tile_pattern.shape[3], bits, cuts)
        H = len(pieces(R))
        tiles_all, tiles_here = tile_pattern.shape[3:]
        Q = T // 2**bits
        f32, b16 = jnp.float32, jnp.bfloat16
        dma = pltpu.SemaphoreType.DMA
        peers = max(C - 1, 1)
        near = 2**bits * C
        anywhere = pl.BlockSpec(memory_space=pl.ANY)
        vmem = pl.BlockSpec(memory_space=pltpu.VMEM)
        results = pl.pallas_call(
            functools.partial(kernel, dims),
            out_shape=(
                pltpu.VMEM((1, m, R), f32),
                pltpu.VMEM((F, R), f32),
            ),
            in_specs=[anywhere] * 4
            + [anywhere] * 3,
            out_specs=(vmem, vmem),
            scratch_shapes=[
                pltpu.SMEM((levels, 1, 2, tiles_here, tiles_all), jnp.int32),
                pltpu.VMEM((m, R), f32),
                pltpu.VMEM((levels, 1, F, m), f32),
                pltpu.VMEM((F, R), f32),
                pltpu.VMEM((levels, 3, block, m), f32),
                pltpu.VMEM((levels, 3, block, m), b16),
                pltpu.VMEM((levels, 3, block, m), b16),
                pltpu.VMEM((levels, R, m), f32),
                pltpu.VMEM((levels, C, R, block), f32),
                pltpu.VMEM((levels, R, block), b16),
                pltpu.VMEM((levels, R, block), b16),
                pltpu.VMEM((levels, 2, R, m), f32),
                pltpu.VMEM((levels, 2, R, m), f32),
                pltpu.VMEM((max(levels - 1, 1), R, m), f32),
                pltpu.VMEM((G, ROWS, LANES), f32),
                pltpu.VMEM((near - 1, G // near, ROWS, LANES), f32),
                pltpu.VMEM((Q, G // near, ROWS, LANES), f32),
                pltpu.VMEM((G, ROWS, LANES), f32),
                dma((levels, 3)),
                dma((4,)),
                dma((QUARTERS,)),
                dma((levels, H, peers)),
                dma((max(levels - 1, 1), H, cuts)),
                dma((levels, H)),
                dma((3,)),
                dma((5,)),
            ],
            compiler_params=pltpu.CompilerParams(
                collective_id=0, has_side_effects=True, vmem_limit_bytes=63 * 2**20
            ),
        )(
            rhs,
            inverse,
            lower,
            upper,
            jnp.swapaxes(tile_pattern, 3, 4),
            tip_coupling,
            tip_rhs,
        )
        return pl.pallas_call(
            store,
            out_shape=(
                jax.ShapeDtypeStruct((1, m, R), f32),
                jax.ShapeDtypeStruct((F, R), f32),
            ),
            in_specs=[anywhere, anywhere],
            out_specs=(anywhere, anywhere),
            scratch_shapes=[dma((2,))],
        )(*(pltpu.with_memory_space_constraint(x, pltpu.VMEM) for x in results))

    return jax.shard_map(
        local,
        mesh=mesh,
        in_specs=(
            P("tm", "col", None),
            P(None, "tm", None, "col"),
            P(None, "tm", None, "col"),
            P(None, "tm", None, "col"),
            P(None, "tm", None, None, "col"),
            P(None, "tm", None, "col"),
            P(),
        ),
        out_specs=(P("tm", "col", None), P()),
        check_vma=False,
    )
```

```python
import contextlib
import functools

import jax
import jax.numpy as jnp
from jax import lax
from jax.experimental import pallas as pl
from jax.experimental.pallas import tpu as pltpu
from jax.sharding import PartitionSpec as P

MESH = pl.DeviceIdType.MESH
LANES = 128
ROWS = 8
TRACE = False
NT = (((1,), (1,)), ((), ()))
NN = (((1,), (0,)), ((), ()))


def scope(name):
    return jax.named_scope(name) if TRACE else contextlib.nullcontext()


def halves_of(x):
    high = x.astype(jnp.bfloat16)
    low = (x - high.astype(jnp.float32)).astype(jnp.bfloat16)
    return high, low


def product(stacked, high, w_high, w_low, form):
    rows = high.shape[0]
    dot = functools.partial(
        lax.dot_general, dimension_numbers=form, preferred_element_type=jnp.float32
    )
    both = dot(stacked, w_high)
    return both[:rows] + both[rows:] + dot(high, w_low)


ORDER = (
    "S00", "P01", "W10", "W11", "J00", "S01", "K00", "W12", "W20", "J01", "W21", "W22",
    "K01", "J02", "P10", "K02", "S10", "J03", "P11", "K03", "S11", "P12", "J10", "S12",
    "K10", "P13", "J11", "S13", "P20", "J12", "S20", "P21", "J13", "S21", "T04", "P22",
    "S22", "T14", "P23", "T23", "S23",
)
SIXTEENTHS = (4, 8, 12, 16)
QUARTERS = 4
PAIRED = (0,)
DIRECT = ()
HALVED = ((0, 0), (0, 1), (0, 2), (0, 3), (1, 0))


def pieces(R):
    ends = [R * e // SIXTEENTHS[-1] for e in SIXTEENTHS]
    return tuple((a, b - a) for a, b in zip([0] + ends, ends))


def kernel(
    dims,
    rhs_hbm,
    inv_hbm,
    low_hbm,
    up_hbm,
    pattern_hbm,
    tip_c_hbm,
    tip_rhs_hbm,
    out,
    tip_out,
    pattern,
    rhs_v,
    tip_c,
    tip_rhs,
    raw,
    w_high,
    w_low,
    cur,
    part,
    s_high,
    s_low,
    send,
    recv,
    joined,
    tip_acc,
    tip_near,
    tip_far,
    tip_all,
    in_sem,
    rhs_sem,
    first_sem,
    part_r,
    join_r,
    row_r,
    tip_r,
    sent,
):
    levels, T, C, block, m, R, F, tiles_all, bits, cuts = dims
    tiles_here = m * tiles_all // block
    tile = block // tiles_all
    N = T * C
    row = lax.axis_index("tm")
    col = lax.axis_index("col")
    me = row * C + col
    groups = F // ROWS
    G = groups * (R // LANES)
    parts = pieces(R)
    H = len(parts)
    last = levels - 1

    sources = (inv_hbm, low_hbm, up_hbm)

    def load(level, kind):
        return pltpu.make_async_copy(
            sources[kind].at[level, 0], raw.at[level, kind], in_sem.at[level, kind]
        )

    def first_load(q):
        rows = pl.ds(q * (block // QUARTERS), block // QUARTERS)
        return pltpu.make_async_copy(
            inv_hbm.at[0, 0, rows], raw.at[0, 0, rows], first_sem.at[q]
        )

    rhs_copy = pltpu.make_async_copy(rhs_hbm.at[0], rhs_v, rhs_sem.at[0])
    pattern_copy = pltpu.make_async_copy(pattern_hbm, pattern, rhs_sem.at[3])
    tip_c_copy = pltpu.make_async_copy(tip_c_hbm, tip_c, rhs_sem.at[1])
    tip_rhs_copy = pltpu.make_async_copy(tip_rhs_hbm, tip_rhs, rhs_sem.at[2])
    rhs_copy.start()
    for q in range(QUARTERS):
        first_load(q).start()
    pattern_copy.start()

    barrier = pltpu.get_barrier_semaphore()

    def greet(device):
        pl.semaphore_signal(barrier, inc=1, device_id=device, device_id_type=MESH)

    near = 2**bits * C
    each = G // near
    Q = T // 2**bits
    place = row // 2**bits
    seat = lax.rem(row, 2**bits) * C + col

    def over(count, action):
        @pl.loop(1, count)
        def _(k):
            action(k)

    def near_of(k):
        other = lax.rem(seat + k, near)
        return other, {"tm": place * 2**bits + other // C, "col": lax.rem(other, C)}

    def far_of(k):
        other = lax.rem(place + k, Q)
        return {"tm": other * 2**bits + lax.rem(row, 2**bits), "col": col}

    by_fours = bits == 2 and levels == 3

    def announce():
        if not by_fours:

            def anyone(k):
                other = lax.rem(me + k, N)
                greet({"tm": other // C, "col": lax.rem(other, C)})

            return over(N, anyone)
        greet({"tm": lax.rem(row + T - 2 + 4 * bit_of(1), T), "col": col})

        @pl.when(bit_of(0) == bit_of(1))
        def _():
            greet({"tm": lax.rem(row + T - 1 + 2 * bit_of(1), T), "col": col})

        over(Q, lambda k: greet(far_of(k)))
        over(near, lambda k: greet(near_of(k)[1]))

    def met():
        if not by_fours:
            return pl.semaphore_wait(barrier, N - 1)
        outer = 1 - lax.rem(bit_of(0) + bit_of(1), 2)
        pl.semaphore_wait(barrier, near + Q - 1 + outer)

    def bit_of(level):
        return lax.rem(row // 2**level, 2)

    announce()

    def split(level, kind):
        if level or kind:
            load(level, kind).wait()
            return split_tiles(level, kind, 0, tiles_all)
        for q in range(QUARTERS):
            first_load(q).wait()
            split_tiles(0, 0, tiles_all * q // QUARTERS, tiles_all * (q + 1) // QUARTERS)

    def split_tiles(level, kind, begin, end):
        @pl.loop(begin, end)
        def _(r):
            rows = pl.ds(pl.multiple_of(r * tile, tile), tile)
            for c in range(tiles_here):
                cols = pl.ds(c * tile, tile)
                w = raw[level, kind, rows, cols]
                if kind:
                    w = w * pattern[level, 0, kind - 1, c, r].astype(jnp.float32)
                high, low = halves_of(w)
                w_high[level, kind, rows, cols] = high
                w_low[level, kind, rows, cols] = low

    def all_of(ref, sem):
        pltpu.make_async_copy(ref, ref, sem).wait()

    def rows_of(h):
        return pl.ds(parts[h][0], parts[h][1])

    def group(level, g):
        width = 2 if level in PAIRED else 1
        return range(g * width, (g + 1) * width)

    def groups_of(level):
        return H // 2 if level in PAIRED else H

    def rows_in(level, g):
        members = group(level, g)
        start = parts[members[0]][0]
        return pl.ds(start, parts[members[-1]][0] + parts[members[-1]][1] - start)

    def part_copy(level, g, k):
        return pltpu.make_async_remote_copy(
            src_ref=part.at[level, 0, rows_in(level, g)],
            dst_ref=part.at[level, k, rows_in(level, g)],
            send_sem=sent.at[0],
            recv_sem=part_r.at[level, g, k - 1],
            device_id={"tm": row, "col": lax.rem(col + k, C)},
            device_id_type=MESH,
        )

    def direct(level, h):
        return level == last or (level, h) in DIRECT

    def cuts_of(level, h):
        return cuts if (level, h) in HALVED and not direct(level, h) else 1

    def span(level, h, q):
        width = m // cuts_of(level, h)
        return pl.ds(q * width, width)

    def row_copy(level, h, way, q):
        stride = 2**level
        at = (rows_of(h), span(level, h, q))
        arrival = row_r.at[level, h]
        if direct(level, h):
            target = lax.rem(row + T - stride + 2 * stride * way, T)
            source = send.at[(level, way, *at)]
        elif isinstance(way, int) and way == 0:
            target = lax.rem(row + T - 2 * stride + 4 * stride * bit_of(level), T)
            source = send.at[(level, bit_of(level), *at)]
            arrival = join_r.at[level, h, q]
        else:
            target = row + stride - 2 * stride * bit_of(level)
            source = joined.at[(level, *at)]
        return pltpu.make_async_remote_copy(
            src_ref=source,
            dst_ref=recv.at[(level, way, *at)],
            send_sem=sent.at[1],
            recv_sem=arrival,
            device_id={"tm": target, "col": col},
            device_id_type=MESH,
        )

    def join(level, h, q):
        row_copy(level, h, 0, q).wait_recv()
        at = (rows_of(h), span(level, h, q))
        joined[(level, *at)] = (
            send[(level, 1 - bit_of(level), *at)] + recv[(level, 0, *at)]
        )
        row_copy(level, h, 1, q).start()

    def settled(level, h):
        ways = pl.ds(0, 2) if direct(level, h) else pl.ds(1, 1)
        all_of(recv.at[level, ways, rows_of(h)], row_r.at[level, h])
        value = cur[level, rows_of(h)] - recv[level, 1, rows_of(h)]
        if direct(level, h):
            value = value - recv[level, 0, rows_of(h)]
        return value

    def solve(level, g):
        if level:
            for h in group(level, g):
                with scope(f"settle{level}{h}"):
                    cur[level, rows_of(h)] = settled(level - 1, h)
        with scope(f"P{level}{g}"):
            rows = rows_in(level, g)
            high, low = halves_of(cur[level, rows])
            stacked = jnp.concatenate([high, low], axis=0)
            part[level, 0, rows] = product(
                stacked, high, w_high[level, 0], w_low[level, 0], NT
            )
        if level == 0 and g == 0:
            with scope("barrier"):
                met()
        for k in range(1, C):
            part_copy(level, g, k).start()

    def add_tip(level, first, end):
        start = parts[first][0]
        n = parts[end - 1][0] + parts[end - 1][1] - start
        mine = pl.ds(pl.multiple_of(col * m, m), m)
        high = s_high[level, pl.ds(start, n), mine]
        low = s_low[level, pl.ds(start, n), mine]
        t_high, t_low = halves_of(tip_c[level, 0])
        dot = functools.partial(
            lax.dot_general, dimension_numbers=NT, preferred_element_type=jnp.float32
        )
        value = dot(t_high, high) + dot(t_high, low) + dot(t_low, high)
        done = 0
        while done < n:
            b, lane = (start + done) // LANES, (start + done) % LANES
            w = min(LANES - lane, n - done)
            piece = value[:, done : done + w].reshape(groups, ROWS, w)
            at = (pl.ds(b * groups, groups), slice(None), pl.ds(lane, w))
            if level == 0:
                tip_acc[at] = piece
            else:
                tip_acc[at] = tip_acc[at] + piece
            done += w

    def spread(level, g):
        rows = rows_in(level, g)
        members = group(level, g)
        closing = level == last and members[-1] == H - 1
        with scope(f"xwait{level}{g}"):
            for k in range(1, C):
                part_copy(level, g, k).wait_recv()
        with scope(f"S{level}{g}"):
            total = part[level, 0, rows]
            for k in range(1, C):
                total = total + part[level, k, rows]
            high, low = halves_of(total)
            s_high[level, rows] = high
            s_low[level, rows] = low
        straight = direct(level, members[0])
        over_end = (row + 2**level) // T
        ways = (over_end, 1 - over_end) if straight else (bit_of(level), 1 - bit_of(level))
        if closing:
            with scope(f"tip{level}{g}"):
                add_tip(level, members[0], H)
                tip_scatter()
        for i in range(2):
            with scope(f"DU{level}{g}"):
                high = s_high[level, rows]
                stacked = jnp.concatenate([high, s_low[level, rows]], axis=0)
                send[level, ways[i], rows] = product(
                    stacked,
                    high,
                    w_high[level, 1 + ways[i]],
                    w_low[level, 1 + ways[i]],
                    NN,
                )
                if not closing and (i == 0 or straight):
                    for h in members:
                        for q in range(cuts_of(level, h)):
                            row_copy(level, h, ways[i] if straight else i, q).start()

    def scatter_copy(k):
        other, device = near_of(k)
        return pltpu.make_async_remote_copy(
            src_ref=tip_acc.at[pl.ds(other * each, each)],
            dst_ref=tip_near.at[k - 1],
            send_sem=sent.at[2],
            recv_sem=tip_r.at[0],
            device_id=device,
            device_id_type=MESH,
        )

    def far_copy(k):
        return pltpu.make_async_remote_copy(
            src_ref=tip_far.at[place],
            dst_ref=tip_far.at[place],
            send_sem=sent.at[3],
            recv_sem=tip_r.at[1],
            device_id=far_of(k),
            device_id_type=MESH,
        )

    def gather_copy(k):
        mine = pl.ds(seat * each, each)
        return pltpu.make_async_remote_copy(
            src_ref=tip_all.at[mine],
            dst_ref=tip_all.at[mine],
            send_sem=sent.at[4],
            recv_sem=tip_r.at[2],
            device_id=near_of(k)[1],
            device_id_type=MESH,
        )

    def tip_scatter():
        over(near, lambda k: scatter_copy(k).start())

    def tip_reduce():
        all_of(tip_near, tip_r.at[0])
        tip_far[place] = tip_acc[pl.ds(seat * each, each)] + jnp.sum(
            tip_near[...], axis=0
        )
        over(Q, lambda k: far_copy(k).start())

    def tip_total():
        all_of(tip_far.at[pl.ds(1, Q - 1)], tip_r.at[1])
        tip_all[pl.ds(seat * each, each)] = jnp.sum(tip_far[...], axis=0)
        over(near, lambda k: gather_copy(k).start())

    def tip_finish():
        all_of(tip_near, tip_r.at[2])
        tip_rhs_copy.wait()
        for b in range(R // LANES):
            lanes = slice(b * LANES, (b + 1) * LANES)
            total = tip_all[b * groups : (b + 1) * groups].reshape(F, LANES)
            tip_out[:, lanes] = tip_rhs[:, lanes] - total

    def final(h):
        start, n = parts[h]
        out[0, :, start : start + n] = settled(last, h).T

    with scope("rhs"):
        rhs_copy.wait()
        for kind in (1, 2):
            load(0, kind).start()
        cur[0] = rhs_v[...].T
    with scope("split00"):
        split(0, 0)
    tip_c_copy.start()
    tip_rhs_copy.start()
    solve(0, 0)
    pattern_copy.wait()
    for kind in (1, 2):
        with scope("split0"):
            split(0, kind)
    for level in range(1, levels):
        for kind in range(3):
            load(level, kind).start()
    tip_c_copy.wait()

    def splits(level, *kinds):
        for kind in kinds:
            with scope(f"split{level}{kind}"):
                split(level, kind)

    def joins(q, level, h):
        if q < cuts_of(level, h) and not direct(level, h):
            with scope(f"join{level}{h}"):
                join(level, h, q)

    def tips(level, end):
        with scope(f"tip{level}{end}"):
            add_tip(level, 0, end)

    def finals(h):
        with scope(f"final{h}"):
            final(h)

    actions = {
        "P": solve,
        "S": spread,
        "J": functools.partial(joins, 0),
        "K": functools.partial(joins, 1),
        "W": splits,
        "T": tips,
    }
    for step in ORDER:
        actions[step[0]](int(step[1]), int(step[2]))
    with scope("tipreduce"):
        tip_reduce()
    over_end = (row + 2**last) // T
    for way in (over_end, 1 - over_end):
        row_copy(last, H - 1, way, 0).start()
    for h in range(H - 2):
        finals(h)
    with scope("tiptotal"):
        tip_total()
    finals(H - 2)
    with scope("tipfinish"):
        tip_finish()
    finals(H - 1)

    with scope("drain"):
        if C > 1:
            all_of(part.at[:, pl.ds(1, C - 1)], sent.at[0])
        all_of(recv, sent.at[1])
        all_of(tip_near, sent.at[2])
        all_of(tip_far.at[pl.ds(1, Q - 1)], sent.at[3])
        all_of(tip_near, sent.at[4])


def store(main, tip, main_out, tip_out, sem):
    copies = [
        pltpu.make_async_copy(main, main_out, sem.at[0]),
        pltpu.make_async_copy(tip, tip_out, sem.at[1]),
    ]
    for copy in copies:
        copy.start()
    for copy in copies:
        copy.wait()


def solution(mesh):
    T, C = mesh.shape["tm"], mesh.shape["col"]

    def local(rhs, inverse, lower, upper, tile_pattern, tip_coupling, tip_rhs):
        levels, _, block, m = inverse.shape
        R = rhs.shape[2]
        F = tip_rhs.shape[0]
        G = (F // ROWS) * (R // LANES)
        cuts = 2 if m % (2 * LANES) == 0 else 1
        bits = 0
        while bits < 2 and G % (2 ** (bits + 1) * C) == 0 and T % 2 ** (bits + 1) == 0:
            bits += 1
        dims = (levels, T, C, block, m, R, F, tile_pattern.shape[3], bits, cuts)
        H = len(pieces(R))
        tiles_all, tiles_here = tile_pattern.shape[3:]
        Q = T // 2**bits
        f32, b16 = jnp.float32, jnp.bfloat16
        dma = pltpu.SemaphoreType.DMA
        peers = max(C - 1, 1)
        near = 2**bits * C
        anywhere = pl.BlockSpec(memory_space=pl.ANY)
        vmem = pl.BlockSpec(memory_space=pltpu.VMEM)
        results = pl.pallas_call(
            functools.partial(kernel, dims),
            out_shape=(
                pltpu.VMEM((1, m, R), f32),
                pltpu.VMEM((F, R), f32),
            ),
            in_specs=[anywhere] * 4
            + [anywhere] * 3,
            out_specs=(vmem, vmem),
            scratch_shapes=[
                pltpu.SMEM((levels, 1, 2, tiles_here, tiles_all), jnp.int32),
                pltpu.VMEM((m, R), f32),
                pltpu.VMEM((levels, 1, F, m), f32),
                pltpu.VMEM((F, R), f32),
                pltpu.VMEM((levels, 3, block, m), f32),
                pltpu.VMEM((levels, 3, block, m), b16),
                pltpu.VMEM((levels, 3, block, m), b16),
                pltpu.VMEM((levels, R, m), f32),
                pltpu.VMEM((levels, C, R, block), f32),
                pltpu.VMEM((levels, R, block), b16),
                pltpu.VMEM((levels, R, block), b16),
                pltpu.VMEM((levels, 2, R, m), f32),
                pltpu.VMEM((levels, 2, R, m), f32),
                pltpu.VMEM((max(levels - 1, 1), R, m), f32),
                pltpu.VMEM((G, ROWS, LANES), f32),
                pltpu.VMEM((near - 1, G // near, ROWS, LANES), f32),
                pltpu.VMEM((Q, G // near, ROWS, LANES), f32),
                pltpu.VMEM((G, ROWS, LANES), f32),
                dma((levels, 3)),
                dma((4,)),
                dma((QUARTERS,)),
                dma((levels, H, peers)),
                dma((max(levels - 1, 1), H, cuts)),
                dma((levels, H)),
                dma((3,)),
                dma((5,)),
            ],
            compiler_params=pltpu.CompilerParams(
                collective_id=0, has_side_effects=True, vmem_limit_bytes=63 * 2**20
            ),
        )(
            rhs,
            inverse,
            lower,
            upper,
            jnp.swapaxes(tile_pattern, 3, 4),
            tip_coupling,
            tip_rhs,
        )
        return pl.pallas_call(
            store,
            out_shape=(
                jax.ShapeDtypeStruct((1, m, R), f32),
                jax.ShapeDtypeStruct((F, R), f32),
            ),
            in_specs=[anywhere, anywhere],
            out_specs=(anywhere, anywhere),
            scratch_shapes=[dma((2,))],
        )(*(pltpu.with_memory_space_constraint(x, pltpu.VMEM) for x in results))

    return jax.shard_map(
        local,
        mesh=mesh,
        in_specs=(
            P("tm", "col", None),
            P(None, "tm", None, "col"),
            P(None, "tm", None, "col"),
            P(None, "tm", None, "col"),
            P(None, "tm", None, None, "col"),
            P(None, "tm", None, "col"),
            P(),
        ),
        out_specs=(P("tm", "col", None), P()),
        check_vma=False,
    )
```

```python
import contextlib
import functools

import jax
import jax.numpy as jnp
from jax import lax
from jax.experimental import pallas as pl
from jax.experimental.pallas import tpu as pltpu
from jax.sharding import PartitionSpec as P

MESH = pl.DeviceIdType.MESH
LANES = 128
ROWS = 8
TRACE = False
NT = (((1,), (1,)), ((), ()))
NN = (((1,), (0,)), ((), ()))


def scope(name):
    return jax.named_scope(name) if TRACE else contextlib.nullcontext()


def halves_of(x):
    high = x.astype(jnp.bfloat16)
    low = (x - high.astype(jnp.float32)).astype(jnp.bfloat16)
    return high, low


def product(stacked, high, w_high, w_low, form):
    rows = high.shape[0]
    dot = functools.partial(
        lax.dot_general, dimension_numbers=form, preferred_element_type=jnp.float32
    )
    both = dot(stacked, w_high)
    return both[:rows] + both[rows:] + dot(high, w_low)


ORDER = (
    "S00", "P01", "W10", "W11", "J00", "S01", "K00", "W12", "W20", "J01", "W21", "W22",
    "K01", "J02", "P10", "K02", "S10", "P11", "J03", "S11", "K03", "P12", "J10", "S12",
    "K10", "P13", "J11", "S13", "K11", "P20", "J12", "S20", "K12", "P21", "J13", "S21",
    "K13", "T04", "P22", "S22", "T14", "P23", "T23", "S23",
)
SIXTEENTHS = (4, 8, 12, 16)
QUARTERS = 4
PAIRED = (0,)
DIRECT = ()
HALVED = tuple((level, piece) for level in (0, 1) for piece in range(4))


def pieces(R):
    ends = [R * e // SIXTEENTHS[-1] for e in SIXTEENTHS]
    return tuple((a, b - a) for a, b in zip([0] + ends, ends))


def kernel(
    dims,
    rhs_hbm,
    inv_hbm,
    low_hbm,
    up_hbm,
    pattern_hbm,
    tip_c_hbm,
    tip_rhs_hbm,
    out,
    tip_out,
    pattern,
    rhs_v,
    tip_c,
    tip_rhs,
    raw,
    w_high,
    w_low,
    cur,
    part,
    s_high,
    s_low,
    send,
    recv,
    joined,
    tip_acc,
    tip_near,
    tip_far,
    tip_all,
    in_sem,
    rhs_sem,
    first_sem,
    part_r,
    join_r,
    row_r,
    tip_r,
    sent,
):
    levels, T, C, block, m, R, F, tiles_all, bits, cuts = dims
    tiles_here = m * tiles_all // block
    tile = block // tiles_all
    N = T * C
    row = lax.axis_index("tm")
    col = lax.axis_index("col")
    me = row * C + col
    groups = F // ROWS
    G = groups * (R // LANES)
    parts = pieces(R)
    H = len(parts)
    last = levels - 1

    sources = (inv_hbm, low_hbm, up_hbm)

    def load(level, kind):
        return pltpu.make_async_copy(
            sources[kind].at[level, 0], raw.at[level, kind], in_sem.at[level, kind]
        )

    def first_load(q):
        rows = pl.ds(q * (block // QUARTERS), block // QUARTERS)
        return pltpu.make_async_copy(
            inv_hbm.at[0, 0, rows], raw.at[0, 0, rows], first_sem.at[q]
        )

    rhs_copy = pltpu.make_async_copy(rhs_hbm.at[0], rhs_v, rhs_sem.at[0])
    pattern_copy = pltpu.make_async_copy(pattern_hbm, pattern, rhs_sem.at[3])
    tip_c_copy = pltpu.make_async_copy(tip_c_hbm, tip_c, rhs_sem.at[1])
    tip_rhs_copy = pltpu.make_async_copy(tip_rhs_hbm, tip_rhs, rhs_sem.at[2])
    rhs_copy.start()
    for q in range(QUARTERS):
        first_load(q).start()
    pattern_copy.start()

    barrier = pltpu.get_barrier_semaphore()

    def greet(device):
        pl.semaphore_signal(barrier, inc=1, device_id=device, device_id_type=MESH)

    near = 2**bits * C
    each = G // near
    Q = T // 2**bits
    place = row // 2**bits
    seat = lax.rem(row, 2**bits) * C + col

    def over(count, action):
        @pl.loop(1, count)
        def _(k):
            action(k)

    def near_of(k):
        other = lax.rem(seat + k, near)
        return other, {"tm": place * 2**bits + other // C, "col": lax.rem(other, C)}

    def far_of(k):
        other = lax.rem(place + k, Q)
        return {"tm": other * 2**bits + lax.rem(row, 2**bits), "col": col}

    by_fours = bits == 2 and levels == 3

    def announce():
        if not by_fours:

            def anyone(k):
                other = lax.rem(me + k, N)
                greet({"tm": other // C, "col": lax.rem(other, C)})

            return over(N, anyone)
        greet({"tm": lax.rem(row + T - 2 + 4 * bit_of(1), T), "col": col})

        @pl.when(bit_of(0) == bit_of(1))
        def _():
            greet({"tm": lax.rem(row + T - 1 + 2 * bit_of(1), T), "col": col})

        over(Q, lambda k: greet(far_of(k)))
        over(near, lambda k: greet(near_of(k)[1]))

    def met():
        if not by_fours:
            return pl.semaphore_wait(barrier, N - 1)
        outer = 1 - lax.rem(bit_of(0) + bit_of(1), 2)
        pl.semaphore_wait(barrier, near + Q - 1 + outer)

    def bit_of(level):
        return lax.rem(row // 2**level, 2)

    announce()

    def split(level, kind):
        if level or kind:
            load(level, kind).wait()
            return split_tiles(level, kind, 0, tiles_all)
        for q in range(QUARTERS):
            first_load(q).wait()
            split_tiles(0, 0, tiles_all * q // QUARTERS, tiles_all * (q + 1) // QUARTERS)

    def split_tiles(level, kind, begin, end):
        @pl.loop(begin, end)
        def _(r):
            rows = pl.ds(pl.multiple_of(r * tile, tile), tile)
            for c in range(tiles_here):
                cols = pl.ds(c * tile, tile)
                w = raw[level, kind, rows, cols]
                if kind:
                    w = w * pattern[level, 0, kind - 1, c, r].astype(jnp.float32)
                high, low = halves_of(w)
                w_high[level, kind, rows, cols] = high
                w_low[level, kind, rows, cols] = low

    def all_of(ref, sem):
        pltpu.make_async_copy(ref, ref, sem).wait()

    def rows_of(h):
        return pl.ds(parts[h][0], parts[h][1])

    def group(level, g):
        width = 2 if level in PAIRED else 1
        return range(g * width, (g + 1) * width)

    def groups_of(level):
        return H // 2 if level in PAIRED else H

    def rows_in(level, g):
        members = group(level, g)
        start = parts[members[0]][0]
        return pl.ds(start, parts[members[-1]][0] + parts[members[-1]][1] - start)

    def part_copy(level, g, k):
        return pltpu.make_async_remote_copy(
            src_ref=part.at[level, 0, rows_in(level, g)],
            dst_ref=part.at[level, k, rows_in(level, g)],
            send_sem=sent.at[0],
            recv_sem=part_r.at[level, g, k - 1],
            device_id={"tm": row, "col": lax.rem(col + k, C)},
            device_id_type=MESH,
        )

    def direct(level, h):
        return level == last or (level, h) in DIRECT

    def cuts_of(level, h):
        return cuts if (level, h) in HALVED and not direct(level, h) else 1

    def span(level, h, q):
        width = m // cuts_of(level, h)
        return pl.ds(q * width, width)

    def row_copy(level, h, way, q):
        stride = 2**level
        at = (rows_of(h), span(level, h, q))
        arrival = row_r.at[level, h]
        if direct(level, h):
            target = lax.rem(row + T - stride + 2 * stride * way, T)
            source = send.at[(level, way, *at)]
        elif isinstance(way, int) and way == 0:
            target = lax.rem(row + T - 2 * stride + 4 * stride * bit_of(level), T)
            source = send.at[(level, bit_of(level), *at)]
            arrival = join_r.at[level, h, q]
        else:
            target = row + stride - 2 * stride * bit_of(level)
            source = joined.at[(level, *at)]
        return pltpu.make_async_remote_copy(
            src_ref=source,
            dst_ref=recv.at[(level, way, *at)],
            send_sem=sent.at[1],
            recv_sem=arrival,
            device_id={"tm": target, "col": col},
            device_id_type=MESH,
        )

    def join(level, h, q):
        row_copy(level, h, 0, q).wait_recv()
        at = (rows_of(h), span(level, h, q))
        joined[(level, *at)] = (
            send[(level, 1 - bit_of(level), *at)] + recv[(level, 0, *at)]
        )
        row_copy(level, h, 1, q).start()

    def settled(level, h):
        ways = pl.ds(0, 2) if direct(level, h) else pl.ds(1, 1)
        all_of(recv.at[level, ways, rows_of(h)], row_r.at[level, h])
        value = cur[level, rows_of(h)] - recv[level, 1, rows_of(h)]
        if direct(level, h):
            value = value - recv[level, 0, rows_of(h)]
        return value

    def solve(level, g):
        if level:
            for h in group(level, g):
                with scope(f"settle{level}{h}"):
                    cur[level, rows_of(h)] = settled(level - 1, h)
        with scope(f"P{level}{g}"):
            rows = rows_in(level, g)
            high, low = halves_of(cur[level, rows])
            stacked = jnp.concatenate([high, low], axis=0)
            part[level, 0, rows] = product(
                stacked, high, w_high[level, 0], w_low[level, 0], NT
            )
        if level == 0 and g == 0:
            with scope("barrier"):
                met()
        for k in range(1, C):
            part_copy(level, g, k).start()

    def add_tip(level, first, end):
        start = parts[first][0]
        n = parts[end - 1][0] + parts[end - 1][1] - start
        mine = pl.ds(pl.multiple_of(col * m, m), m)
        high = s_high[level, pl.ds(start, n), mine]
        low = s_low[level, pl.ds(start, n), mine]
        t_high, t_low = halves_of(tip_c[level, 0])
        dot = functools.partial(
            lax.dot_general, dimension_numbers=NT, preferred_element_type=jnp.float32
        )
        value = dot(t_high, high) + dot(t_high, low) + dot(t_low, high)
        done = 0
        while done < n:
            b, lane = (start + done) // LANES, (start + done) % LANES
            w = min(LANES - lane, n - done)
            piece = value[:, done : done + w].reshape(groups, ROWS, w)
            at = (pl.ds(b * groups, groups), slice(None), pl.ds(lane, w))
            if level == 0:
                tip_acc[at] = piece
            else:
                tip_acc[at] = tip_acc[at] + piece
            done += w

    def spread(level, g):
        rows = rows_in(level, g)
        members = group(level, g)
        closing = level == last and members[-1] == H - 1
        with scope(f"xwait{level}{g}"):
            for k in range(1, C):
                part_copy(level, g, k).wait_recv()
        with scope(f"S{level}{g}"):
            total = part[level, 0, rows]
            for k in range(1, C):
                total = total + part[level, k, rows]
            high, low = halves_of(total)
            s_high[level, rows] = high
            s_low[level, rows] = low
        straight = direct(level, members[0])
        over_end = (row + 2**level) // T
        ways = (over_end, 1 - over_end) if straight else (bit_of(level), 1 - bit_of(level))
        if closing:
            with scope(f"tip{level}{g}"):
                add_tip(level, members[0], H)
                tip_scatter()
        for i in range(2):
            with scope(f"DU{level}{g}"):
                high = s_high[level, rows]
                stacked = jnp.concatenate([high, s_low[level, rows]], axis=0)
                send[level, ways[i], rows] = product(
                    stacked,
                    high,
                    w_high[level, 1 + ways[i]],
                    w_low[level, 1 + ways[i]],
                    NN,
                )
                if not closing and (i == 0 or straight):
                    for h in members:
                        for q in range(cuts_of(level, h)):
                            row_copy(level, h, ways[i] if straight else i, q).start()

    def scatter_copy(k):
        other, device = near_of(k)
        return pltpu.make_async_remote_copy(
            src_ref=tip_acc.at[pl.ds(other * each, each)],
            dst_ref=tip_near.at[k - 1],
            send_sem=sent.at[2],
            recv_sem=tip_r.at[0],
            device_id=device,
            device_id_type=MESH,
        )

    def far_copy(k):
        return pltpu.make_async_remote_copy(
            src_ref=tip_far.at[place],
            dst_ref=tip_far.at[place],
            send_sem=sent.at[3],
            recv_sem=tip_r.at[1],
            device_id=far_of(k),
            device_id_type=MESH,
        )

    def gather_copy(k):
        mine = pl.ds(seat * each, each)
        return pltpu.make_async_remote_copy(
            src_ref=tip_all.at[mine],
            dst_ref=tip_all.at[mine],
            send_sem=sent.at[4],
            recv_sem=tip_r.at[2],
            device_id=near_of(k)[1],
            device_id_type=MESH,
        )

    def tip_scatter():
        over(near, lambda k: scatter_copy(k).start())

    def tip_reduce():
        all_of(tip_near, tip_r.at[0])
        tip_far[place] = tip_acc[pl.ds(seat * each, each)] + jnp.sum(
            tip_near[...], axis=0
        )
        over(Q, lambda k: far_copy(k).start())

    def tip_total():
        all_of(tip_far.at[pl.ds(1, Q - 1)], tip_r.at[1])
        tip_all[pl.ds(seat * each, each)] = jnp.sum(tip_far[...], axis=0)
        over(near, lambda k: gather_copy(k).start())

    def tip_finish():
        all_of(tip_near, tip_r.at[2])
        tip_rhs_copy.wait()
        for b in range(R // LANES):
            lanes = slice(b * LANES, (b + 1) * LANES)
            total = tip_all[b * groups : (b + 1) * groups].reshape(F, LANES)
            tip_out[:, lanes] = tip_rhs[:, lanes] - total

    def final(h):
        start, n = parts[h]
        out[0, :, start : start + n] = settled(last, h).T

    with scope("rhs"):
        rhs_copy.wait()
        for kind in (1, 2):
            load(0, kind).start()
        cur[0] = rhs_v[...].T
    with scope("split00"):
        split(0, 0)
    tip_c_copy.start()
    tip_rhs_copy.start()
    solve(0, 0)
    pattern_copy.wait()
    for kind in (1, 2):
        with scope("split0"):
            split(0, kind)
    for level in range(1, levels):
        for kind in range(3):
            load(level, kind).start()
    tip_c_copy.wait()

    def splits(level, *kinds):
        for kind in kinds:
            with scope(f"split{level}{kind}"):
                split(level, kind)

    def joins(q, level, h):
        if q < cuts_of(level, h) and not direct(level, h):
            with scope(f"join{level}{h}"):
                join(level, h, q)

    def tips(level, end):
        with scope(f"tip{level}{end}"):
            add_tip(level, 0, end)

    def finals(h):
        with scope(f"final{h}"):
            final(h)

    actions = {
        "P": solve,
        "S": spread,
        "J": functools.partial(joins, 0),
        "K": functools.partial(joins, 1),
        "W": splits,
        "T": tips,
    }
    for step in ORDER:
        actions[step[0]](int(step[1]), int(step[2]))
    with scope("tipreduce"):
        tip_reduce()
    over_end = (row + 2**last) // T
    for way in (over_end, 1 - over_end):
        row_copy(last, H - 1, way, 0).start()
    for h in range(H - 2):
        finals(h)
    with scope("tiptotal"):
        tip_total()
    finals(H - 2)
    with scope("tipfinish"):
        tip_finish()
    finals(H - 1)

    with scope("drain"):
        if C > 1:
            all_of(part.at[:, pl.ds(1, C - 1)], sent.at[0])
        all_of(recv, sent.at[1])
        all_of(tip_near, sent.at[2])
        all_of(tip_far.at[pl.ds(1, Q - 1)], sent.at[3])
        all_of(tip_near, sent.at[4])


def store(main, tip, main_out, tip_out, sem):
    copies = [
        pltpu.make_async_copy(main, main_out, sem.at[0]),
        pltpu.make_async_copy(tip, tip_out, sem.at[1]),
    ]
    for copy in copies:
        copy.start()
    for copy in copies:
        copy.wait()


def solution(mesh):
    T, C = mesh.shape["tm"], mesh.shape["col"]

    def local(rhs, inverse, lower, upper, tile_pattern, tip_coupling, tip_rhs):
        levels, _, block, m = inverse.shape
        R = rhs.shape[2]
        F = tip_rhs.shape[0]
        G = (F // ROWS) * (R // LANES)
        cuts = 2 if m % (2 * LANES) == 0 else 1
        bits = 0
        while bits < 2 and G % (2 ** (bits + 1) * C) == 0 and T % 2 ** (bits + 1) == 0:
            bits += 1
        dims = (levels, T, C, block, m, R, F, tile_pattern.shape[3], bits, cuts)
        H = len(pieces(R))
        tiles_all, tiles_here = tile_pattern.shape[3:]
        Q = T // 2**bits
        f32, b16 = jnp.float32, jnp.bfloat16
        dma = pltpu.SemaphoreType.DMA
        peers = max(C - 1, 1)
        near = 2**bits * C
        anywhere = pl.BlockSpec(memory_space=pl.ANY)
        vmem = pl.BlockSpec(memory_space=pltpu.VMEM)
        results = pl.pallas_call(
            functools.partial(kernel, dims),
            out_shape=(
                pltpu.VMEM((1, m, R), f32),
                pltpu.VMEM((F, R), f32),
            ),
            in_specs=[anywhere] * 4
            + [anywhere] * 3,
            out_specs=(vmem, vmem),
            scratch_shapes=[
                pltpu.SMEM((levels, 1, 2, tiles_here, tiles_all), jnp.int32),
                pltpu.VMEM((m, R), f32),
                pltpu.VMEM((levels, 1, F, m), f32),
                pltpu.VMEM((F, R), f32),
                pltpu.VMEM((levels, 3, block, m), f32),
                pltpu.VMEM((levels, 3, block, m), b16),
                pltpu.VMEM((levels, 3, block, m), b16),
                pltpu.VMEM((levels, R, m), f32),
                pltpu.VMEM((levels, C, R, block), f32),
                pltpu.VMEM((levels, R, block), b16),
                pltpu.VMEM((levels, R, block), b16),
                pltpu.VMEM((levels, 2, R, m), f32),
                pltpu.VMEM((levels, 2, R, m), f32),
                pltpu.VMEM((max(levels - 1, 1), R, m), f32),
                pltpu.VMEM((G, ROWS, LANES), f32),
                pltpu.VMEM((near - 1, G // near, ROWS, LANES), f32),
                pltpu.VMEM((Q, G // near, ROWS, LANES), f32),
                pltpu.VMEM((G, ROWS, LANES), f32),
                dma((levels, 3)),
                dma((4,)),
                dma((QUARTERS,)),
                dma((levels, H, peers)),
                dma((max(levels - 1, 1), H, cuts)),
                dma((levels, H)),
                dma((3,)),
                dma((5,)),
            ],
            compiler_params=pltpu.CompilerParams(
                collective_id=0, has_side_effects=True, vmem_limit_bytes=63 * 2**20
            ),
        )(
            rhs,
            inverse,
            lower,
            upper,
            jnp.swapaxes(tile_pattern, 3, 4),
            tip_coupling,
            tip_rhs,
        )
        return pl.pallas_call(
            store,
            out_shape=(
                jax.ShapeDtypeStruct((1, m, R), f32),
                jax.ShapeDtypeStruct((F, R), f32),
            ),
            in_specs=[anywhere, anywhere],
            out_specs=(anywhere, anywhere),
            scratch_shapes=[dma((2,))],
        )(*(pltpu.with_memory_space_constraint(x, pltpu.VMEM) for x in results))

    return jax.shard_map(
        local,
        mesh=mesh,
        in_specs=(
            P("tm", "col", None),
            P(None, "tm", None, "col"),
            P(None, "tm", None, "col"),
            P(None, "tm", None, "col"),
            P(None, "tm", None, None, "col"),
            P(None, "tm", None, "col"),
            P(),
        ),
        out_specs=(P("tm", "col", None), P()),
        check_vma=False,
    )
```
